1024 devices in a mesh: gz: 16 (over y, core), xy: 64 (over z, x).
Axes of the slice: x: 4, y: 8, z: 16, core: 2. Of those that a mesh axis runs over, the one named last changes fastest.
Arguments:
- density: float32 [128, 8192, 128], P('gz', 'xy'), may hold values from -96 to 96
- live_slices: int32 [16, 64], replicated, may hold values from 1 to 8, as said below
- shear_slopes: float32 [2], replicated, may hold values from -0.12 to 0.12
- palette: float32 [3], replicated, may hold values from 0.5 to 2
- depth_order: int32 [2, 16], replicated, may hold values from 0 to 15, each once within a row
- tile_owner: int32 [2, 16], replicated, may hold values from 0 to 15, each once within a row
Outputs:
- owned_tiles: float32 [2, 4, 16, 512, 128], P(None, None, 'gz', 'xy')
The draws below stay inside these ranges and needn't reach their ends.
Inputs may be any that keep to these rules, and one draw needn't show every extreme that they name: `live_slices`: some brick has all 8 slices live. `depth_order`: each row lists every slab once. `tile_owner`: each row names every index of gz once.
All inputs are finite; a program needn't handle non-finite values.
Results may differ from the reference program's by a relative error of at most 0.00042.
Values may be sent and summed in bfloat16 or wider, within the bound.
A program may use at most 32 MiB of HBM per device.

```python
import math
from functools import partial
import jax
import jax.numpy as jnp
from jax import lax

CZ = 8
CY = 128
W = 128
NZ = 128
NY = 8192
TR = 8
N_GZ = 16
N_XY = 64


def draw_live_slices(key, part):
    spread = jax.random.randint(jax.random.fold_in(key, 11), (N_GZ, N_XY), 1, CZ + 1)
    chosen = jax.random.randint(jax.random.fold_in(key, 12), (), 0, N_GZ * N_XY)
    flat_index = jnp.arange(N_GZ * N_XY).reshape(N_GZ, N_XY)
    return jnp.where(flat_index == chosen, CZ, spread).astype(jnp.int32)


def draw_density(key, part):
    shape = (NZ, NY, W)
    return 16.0 * jax.random.truncated_normal(jax.random.fold_in(key, 23), -6.0, 6.0, shape, jnp.float32)


def setup_inputs(seed: int = 0) -> dict:
    keys = jax.random.split(jax.random.key(seed), 7)
    density = draw_density(jax.random.fold_in(keys[6], 71), 0)
    live_slices = draw_live_slices(jax.random.fold_in(keys[6], 71), 0)
    shear_slopes = jnp.clip(jax.random.uniform(keys[2], (2,), jnp.float32, -0.12, 0.12), -0.12, 0.12)
    palette = jnp.clip(jnp.exp(jax.random.uniform(keys[3], (3,), jnp.float32, math.log(0.5), math.log(2.0))), 0.5, 2.0)
    depth_order = jax.vmap(lambda own: jax.random.permutation(own, N_GZ))(jax.random.split(keys[4], 2)).reshape((2, N_GZ)).astype(jnp.int32)
    tile_owner = jax.vmap(lambda own: jax.random.permutation(own, N_GZ))(jax.random.split(keys[5], 2)).reshape((2, N_GZ)).astype(jnp.int32)
    return {"density": density, "live_slices": live_slices, "shear_slopes": shear_slopes, "palette": palette, "depth_order": depth_order, "tile_owner": tile_owner}


TAPS = (1.0 / 9,) * 9
LIGHT = (0.48, 0.6, 0.64)

def smooth_along(volume, along):
    extent = volume.shape[along] - 8
    total = TAPS[0] * lax.slice_in_dim(volume, 0, extent, axis=along)
    for offset in range(1, 9):
        total = total + TAPS[offset] * lax.slice_in_dim(volume, offset, offset + extent, axis=along)
    return total

def smooth_all(volume):
    return smooth_along(smooth_along(smooth_along(volume, 0), 1), 2)

def shade(padded, live_mask, palette, extinct, stack_axis):
    center = padded[1:-1, 1:-1, 1:-1]
    diff_depth = 0.5 * (padded[2:, 1:-1, 1:-1] - padded[:-2, 1:-1, 1:-1])
    diff_rows = 0.5 * (padded[1:-1, 2:, 1:-1] - padded[1:-1, :-2, 1:-1])
    diff_cols = 0.5 * (padded[1:-1, 1:-1, 2:] - padded[1:-1, 1:-1, :-2])
    magnitude = jnp.sqrt(diff_depth * diff_depth + diff_rows * diff_rows + diff_cols * diff_cols + 0.01)
    facing = jnp.maximum(0.0, LIGHT[0] * diff_depth + LIGHT[1] * diff_rows + LIGHT[2] * diff_cols) / magnitude
    opacity = jnp.where(live_mask, 1.0 - jnp.exp(-extinct * jax.nn.softplus(2.0 * center)), 0.0)
    bright = opacity * (0.25 + 0.75 * facing)
    stacked = jnp.stack([bright * palette[0], bright * palette[1], bright * palette[2], opacity], axis=stack_axis)
    return stacked.astype(jnp.bfloat16)

def shear_matrix(shear_slope, slice_depth, columns, total_depth):
    shift = shear_slope * (slice_depth + 0.5 - 0.5 * total_depth)
    shift = shift[..., None, None]
    source = lax.broadcasted_iota(jnp.float32, (columns, columns), 0)
    target = lax.broadcasted_iota(jnp.float32, (columns, columns), 1)
    return jnp.maximum(0.0, 1.0 - jnp.abs(source - target + shift)).astype(jnp.bfloat16)

def composite(fragments, order_row):
    ordered = jnp.take(fragments, order_row, axis=0)

    def blend(carry, fragment):
        shaded, transmit = carry
        return ((shaded + transmit * fragment[:3], transmit * (1.0 - fragment[3])), None)
    plane = fragments.shape[2:]
    init = (jnp.zeros((3,) + plane, jnp.float32), jnp.ones(plane, jnp.float32))
    (shaded, transmit), _ = lax.scan(blend, init, ordered)
    return jnp.concatenate([shaded, (1.0 - transmit)[None]], axis=0)

def render_column(column_index, padded_all, live_slices, shear_slopes, palette, depth_order):
    extinct = 3.0 / NZ
    start = (column_index * CY).astype(jnp.int32)
    zero = jnp.zeros((), jnp.int32)
    column_block = lax.dynamic_slice(padded_all, (zero, start, zero), (NZ + 10, CY + 10, W + 10))
    smoothed = smooth_all(column_block)
    depth_pos = lax.broadcasted_iota(jnp.int32, (NZ + 2, 1, 1), 0)
    row_pos = start - 1 + lax.broadcasted_iota(jnp.int32, (1, CY + 2, 1), 1)
    col_pos = lax.broadcasted_iota(jnp.int32, (1, 1, W + 2), 2)
    keep = (depth_pos >= 1) & (depth_pos <= NZ) & (row_pos >= 0) & (row_pos < NY) & (col_pos >= 1) & (col_pos <= W)
    padded = jnp.where(keep, smoothed, 0.0)
    live_column = lax.dynamic_index_in_dim(live_slices, column_index, axis=1, keepdims=False)
    local_depth = lax.broadcasted_iota(jnp.int32, (N_GZ, CZ), 1)
    live_mask = (local_depth < live_column[:, None]).reshape(NZ, 1, 1)
    rgba = shade(padded, live_mask, palette, extinct, 0)
    slabs = rgba.reshape(4, N_GZ, CZ, CY, W).transpose(2, 1, 0, 3, 4)
    slab_start = (lax.broadcasted_iota(jnp.int32, (N_GZ,), 0) * CZ).astype(jnp.float32)
    images = []
    for view_index in range(2):

        def march(carry, item):
            shaded, transmit = carry
            layer, local = item
            matrix = shear_matrix(shear_slopes[view_index], slab_start + local.astype(jnp.float32), W, NZ)
            sheared = jnp.einsum('gcyw,gwx->gcyx', layer.astype(jnp.float32), matrix.astype(jnp.float32), precision=lax.Precision.HIGHEST)
            return ((shaded + transmit[:, None] * sheared[:, :3], transmit * (1.0 - sheared[:, 3])), None)
        init = (jnp.zeros((N_GZ, 3, CY, W), jnp.float32), jnp.ones((N_GZ, CY, W), jnp.float32))
        depths = lax.broadcasted_iota(jnp.int32, (CZ,), 0)
        (shaded, transmit), _ = lax.scan(march, init, (slabs, depths), reverse=view_index == 1)
        fragments = jnp.concatenate([shaded, (1.0 - transmit)[:, None]], axis=1)
        images.append(composite(fragments, depth_order[view_index]))
    return jnp.stack(images)

def reference(density, live_slices, shear_slopes, palette, depth_order, tile_owner):
    padded_all = jnp.pad(density, 5)
    render = partial(render_column, padded_all=padded_all, live_slices=live_slices, shear_slopes=shear_slopes, palette=palette, depth_order=depth_order)
    images = lax.map(render, lax.broadcasted_iota(jnp.int32, (N_XY,), 0))
    tiles = images.reshape(N_XY, 2, 4, N_GZ, TR, W)
    ranks = lax.broadcasted_iota(jnp.int32, (N_GZ,), 0)
    inverse = lax.optimization_barrier(jnp.sum(ranks[None, None, :] * (tile_owner[:, None, :] == ranks[None, :, None]).astype(jnp.int32), axis=2))
    owned = []
    for view_index in range(2):
        picked = jnp.take(tiles[:, view_index], inverse[view_index], axis=2)
        owned.append(picked.transpose(1, 2, 0, 3, 4).reshape(4, N_GZ, N_XY * TR, W))
    return jnp.stack(owned)
```

```python
import functools

import jax
import jax.numpy as jnp
from jax import lax
from jax.experimental import pallas as pl
from jax.experimental.pallas import tpu as pltpu
from jax.sharding import PartitionSpec as P

LIGHT = (0.48, 0.6, 0.64)
LOG2E = 1.4426950408889634
CHUNKS = ((0, 32), (32, 64), (64, 96), (96, 128))
F32, BF16 = jnp.float32, jnp.bfloat16


def spread(first, second, inside):
    return jnp.where(inside, jnp.where((first - second <= 4) & (second - first <= 4), 1.0, 0.0), 0.0)


def kernel(
    G, R, depth_axis, row_axis,
    live_ref, slopes_ref, palette_ref, order_ref, owner_ref, dens_ref,
    out_ref,
    ext, summed, rowed, smooth, dcol, band, layers, shear, sheared, outbox, inbox, inverse,
    local_sem, zsend, zrecv, rsend, rrecv, tsend, trecv,
):
    me = lax.axis_index(depth_axis)
    col = lax.axis_index(row_axis)
    CZ, CY, W = dens_ref.shape
    TR = CY // G
    NC = len(CHUNKS)
    has = {-1: me > 0, 1: me < G - 1}
    hasr = {-1: col > 0, 1: col < R - 1}
    at = lambda g, r: {depth_axis: g, row_axis: r}

    barrier = pltpu.get_barrier_semaphore()

    def greet(k, carry):
        pl.semaphore_signal(barrier, inc=1, device_id=at(lax.rem(me + k, G), col))
        return carry

    lax.fori_loop(1, G, greet, 0)
    for dr in (-1, 1):
        for dz in (-1, 0, 1):
            ok = hasr[dr] if dz == 0 else hasr[dr] & has[dz]

            @pl.when(ok)
            def _():
                pl.semaphore_signal(barrier, inc=1, device_id=at(me + dz, col + dr))

    local = pltpu.make_async_copy(dens_ref, ext.at[5:13, 8:136, :], local_sem)
    local.start()
    beside = hasr[-1].astype(jnp.int32) + hasr[1].astype(jnp.int32)
    above = has[-1].astype(jnp.int32) + has[1].astype(jnp.int32)
    pl.semaphore_wait(barrier, (G - 1) + beside * (1 + above))

    def zcopy(dz, k):
        lo, hi = CHUNKS[k]
        src = dens_ref.at[3:8, lo:hi, :] if dz == 1 else dens_ref.at[0:5, lo:hi, :]
        dst = ext.at[0:5, 8 + lo : 8 + hi, :] if dz == 1 else ext.at[13:18, 8 + lo : 8 + hi, :]
        side = (dz + 1) // 2
        return pltpu.make_async_remote_copy(
            src, dst, zsend.at[side, k], zrecv.at[side, k], device_id=at(me + dz, col)
        )

    def rcopy(dz, dr):
        zs, zd = {0: (slice(0, 8), slice(5, 13)), 1: (slice(3, 8), slice(0, 5)), -1: (slice(0, 5), slice(13, 18))}[dz]
        rs, rd = {1: (slice(120, 128), slice(0, 8)), -1: (slice(0, 8), slice(136, 144))}[dr]
        side = (dr + 1) // 2
        return pltpu.make_async_remote_copy(
            dens_ref.at[zs, rs, :], ext.at[zd, rd, :], rsend.at[side, dz + 1], rrecv.at[side, dz + 1],
            device_id=at(me + dz, col + dr),
        )

    zcopies = [(dz, k) for k in range(NC) for dz in (1, -1)]
    rcopies = [(dz, dr) for dr in (-1, 1) for dz in (1, -1, 0)]

    def allowed(dz, dr):
        return hasr[dr] if dz == 0 else hasr[dr] & has[dz]

    for dz in (1, -1):
        @pl.when(has[dz])
        def _():
            zcopy(dz, 0).start()
    for dz, dr in rcopies:
        @pl.when(allowed(dz, dr))
        def _():
            rcopy(dz, dr).start()
    for dz in (1, -1):
        @pl.when(has[dz])
        def _():
            for k in range(1, NC):
                zcopy(dz, k).start()

    for dz in (1, -1):
        @pl.when(jnp.logical_not(has[-dz]))
        def _():
            zd = slice(0, 5) if dz == 1 else slice(13, 18)
            ext[zd, :, :] = jnp.zeros((5, CY + 16, W), F32)
    for dr in (1, -1):
        @pl.when(jnp.logical_not(hasr[-dr]))
        def _():
            rd = slice(0, 8) if dr == 1 else slice(136, 144)
            ext[:, rd, :] = jnp.zeros((CZ + 10, 8, W), F32)

    def invert(d, carry):
        for v in range(2):
            found = jnp.int32(0)
            for t in range(G):
                found = jnp.maximum(found, t * (owner_ref[v, t] == d).astype(jnp.int32))
            inverse[v, d] = found
        return carry

    lax.fori_loop(0, G, invert, 0)

    source = lax.broadcasted_iota(jnp.int32, (W, W), 0)
    target = lax.broadcasted_iota(jnp.int32, (W, W), 1)
    ones = spread(source, target, True)
    diff = spread(source, target + 1, target + 1 < W) - spread(source, target - 1, target >= 1)
    for half in range(2):
        band[half * W : half * W + W, 0:W] = ones.astype(BF16)
        band[half * W : half * W + W, W : 2 * W] = diff.astype(BF16)

    offset = (source - target).astype(F32)

    def shears(z, carry):
        depth = (me * CZ + z).astype(F32) + (0.5 - 0.5 * CZ * G)
        for v in range(2):
            m = jnp.maximum(0.0, 1.0 - jnp.abs(offset + slopes_ref[v] * depth))
            shear[z, :, v * W : v * W + W] = m.astype(BF16)
        return carry

    lax.fori_loop(0, CZ, shears, 0)

    live = live_ref[me, col]
    brightest = jnp.maximum(jnp.maximum(palette_ref[0], palette_ref[1]), palette_ref[2])

    def depth_sums(lo, hi):
        def block(b, carry):
            rows = pl.ds(pl.multiple_of(lo + 8 * b, 8), 8)
            x = [ext[z, rows, :] for z in range(CZ + 10)]
            two = [x[i] + x[i + 1] for i in range(CZ + 8)]
            four = [two[i] + two[i + 2] for i in range(CZ + 6)]
            eight = [four[i] + four[i + 4] for i in range(CZ + 2)]
            for z in range(CZ + 2):
                summed[z, rows, :] = eight[z] + x[z + 8]
            return carry

        lax.fori_loop(0, (hi - lo) // 8, block, 0)

    def smooth_rows(lo, hi):
        def layer(z, carry):
            for j in range(lo, hi, 8):
                s = [summed[z, j + k : j + 8 + k, :] for k in range(9)]
                rowed[z, j : j + 8, :] = (
                    ((s[0] + s[1]) + (s[2] + s[3])) + ((s[4] + s[5]) + (s[6] + s[7])) + s[8]
                )
            return carry

        lax.fori_loop(0, CZ + 2, layer, 0)

    def smooth_cols(lo, hi):
        def layer(z, carry):
            x = rowed[z, lo:hi, :]
            high = x.astype(BF16)
            low = (x - high.astype(F32)).astype(BF16)
            both = jnp.dot(
                jnp.concatenate([high, low], axis=1), band[...], preferred_element_type=F32
            )
            smooth[z, lo:hi, :] = both[:, 0:W]
            dcol[z, lo:hi, :] = both[:, W : 2 * W]
            return carry

        lax.fori_loop(0, CZ + 2, layer, 0)

    def shade(lo, hi):
        def layer(z, carry):
            alive = (z < live).astype(jnp.int32).astype(F32)
            bright_of = alive * brightest
            for r in range(lo, hi, 16):
                q = r + 4
                n = 16
                center = smooth[z + 1, q : q + n, :]
                dz = smooth[z + 2, q : q + n, :] - smooth[z, q : q + n, :]
                dr = smooth[z + 1, q + 1 : q + n + 1, :] - smooth[z + 1, q - 1 : q + n - 1, :]
                dc = dcol[z + 1, q : q + n, :]
                along = jnp.maximum(0.0, LIGHT[0] * dz + LIGHT[1] * dr + LIGHT[2] * dc)
                facing = along * lax.rsqrt(dz * dz + dr * dr + dc * dc + 0.01 * 1458.0 * 1458.0)
                y = center * (2.0 / 729.0)
                soft = jnp.maximum(y, 0.0) + jnp.log(1.0 + jnp.exp(-jnp.abs(y)))
                opacity = 1.0 - jnp.exp(soft * (-3.0 / (CZ * G)))
                layers[z, 0, r : r + n, :] = (opacity * (0.25 + 0.75 * facing) * bright_of).astype(BF16)
                layers[z, 1, r : r + n, :] = (opacity * alive).astype(BF16)
            return carry

        lax.fori_loop(0, CZ, layer, 0)

    def shear_rows(lo, hi):
        def layer(z, carry):
            lhs = layers[z, :, lo:hi, :].reshape(2 * (hi - lo), W)
            out = jnp.dot(lhs, shear[z], preferred_element_type=F32)
            sheared[z, :, lo // TR : hi // TR] = out.reshape(2, (hi - lo) // TR, TR, 2 * W)
            return carry

        lax.fori_loop(0, CZ, layer, 0)

    def clear(lo, hi):
        for dz in (-1, 1):
            @pl.when(jnp.logical_not(has[dz]))
            def _():
                smooth[0 if dz == -1 else CZ + 1, lo:hi, :] = jnp.zeros((hi - lo, W), F32)

    local.wait()
    for dz, dr in rcopies:
        @pl.when(allowed(-dz, -dr))
        def _():
            rcopy(dz, dr).wait_recv()

    depth_sums(0, 8)
    depth_sums(CY + 8, CY + 16)
    done_rows, done_smooth = 0, 0
    for k in range(NC):
        for dz in (1, -1):
            @pl.when(has[-dz])
            def _():
                zcopy(dz, k).wait_recv()
        lo, hi = CHUNKS[k]
        depth_sums(8 + lo, 8 + hi)
        last = k == NC - 1
        upto = CY + 8 if last else hi
        smooth_rows(done_smooth, upto)
        smooth_cols(done_smooth, upto)
        clear(done_smooth, upto)
        if k == 0:
            @pl.when(jnp.logical_not(hasr[-1]))
            def _():
                smooth[:, 0:4, :] = jnp.zeros((CZ + 2, 4, W), F32)
        if last:
            @pl.when(jnp.logical_not(hasr[1]))
            def _():
                smooth[:, CY + 4 : CY + 8, :] = jnp.zeros((CZ + 2, 4, W), F32)
        done_smooth = upto
        shaded = CY if last else hi - 16
        shade(done_rows, shaded)
        shear_rows(done_rows, shaded)
        done_rows = shaded

    def tcopy(d):
        return pltpu.make_async_remote_copy(
            outbox.at[d], inbox.at[me], tsend.at[d], trecv.at[me], device_id=at(d, col)
        )

    def march(d, box, slot):
        for v in range(2):
            tile = inverse[v, d]
            shaded, transmit = None, None
            for z in range(CZ) if v == 0 else range(CZ - 1, -1, -1):
                b = sheared[z, 0, tile, :, v * W : v * W + W]
                a = sheared[z, 1, tile, :, v * W : v * W + W]
                shaded = b if shaded is None else shaded + transmit * b
                transmit = 1.0 - a if transmit is None else transmit * (1.0 - a)
            box[slot, v, 0] = shaded
            box[slot, v, 1] = transmit

    def send(k, carry):
        d = lax.rem(me + k, G)
        march(d, outbox, d)
        tcopy(d).start()
        return carry

    lax.fori_loop(1, G, send, 0)
    march(me, inbox, me)

    def receive(k, carry):
        s = lax.rem(me + G - k, G)
        pltpu.make_async_remote_copy(
            outbox.at[s], inbox.at[s], tsend.at[s], trecv.at[s], device_id=at(s, col)
        ).wait_recv()
        return carry

    lax.fori_loop(1, G, receive, 0)

    for v in range(2):
        def blend(i, carry):
            shaded, transmit = carry
            s = order_ref[v, i]
            return shaded + transmit * inbox[s, v, 0], transmit * inbox[s, v, 1]

        shaded, transmit = lax.fori_loop(
            0, G, blend, (jnp.zeros((TR, W), F32), jnp.ones((TR, W), F32)), unroll=True
        )
        for c in range(3):
            out_ref[v, c] = shaded * (palette_ref[c] / brightest)
        out_ref[v, 3] = 1.0 - transmit

    for dz in (1, -1):
        @pl.when(has[dz])
        def _():
            for k in range(NC):
                zcopy(dz, k).wait_send()
    for dz, dr in rcopies:
        @pl.when(allowed(dz, dr))
        def _():
            rcopy(dz, dr).wait_send()

    def sent(k, carry):
        d = lax.rem(me + k, G)
        tcopy(d).wait_send()
        return carry

    lax.fori_loop(1, G, sent, 0)


def solution(mesh):
    depth_axis, row_axis = mesh.axis_names
    G, R = mesh.shape[depth_axis], mesh.shape[row_axis]

    def body(density, live_slices, shear_slopes, palette, depth_order, tile_owner):
        CZ, CY, W = density.shape
        TR = CY // G
        smem = pl.BlockSpec(memory_space=pltpu.SMEM)
        dma = pltpu.SemaphoreType.DMA
        NC = len(CHUNKS)
        out = pl.pallas_call(
            functools.partial(kernel, G, R, depth_axis, row_axis),
            out_shape=jax.ShapeDtypeStruct((2, 4, TR, W), F32),
            in_specs=[smem] * 5 + [pl.BlockSpec(memory_space=pl.ANY)],
            out_specs=pl.BlockSpec(memory_space=pltpu.VMEM),
            scratch_shapes=[
                pltpu.VMEM((CZ + 10, CY + 16, W), F32),
                pltpu.VMEM((CZ + 2, CY + 16, W), F32),
                pltpu.VMEM((CZ + 2, CY + 8, W), F32),
                pltpu.VMEM((CZ + 2, CY + 8, W), F32),
                pltpu.VMEM((CZ + 2, CY + 8, W), F32),
                pltpu.VMEM((2 * W, 2 * W), BF16),
                pltpu.VMEM((CZ, 2, CY, W), BF16),
                pltpu.VMEM((CZ, W, 2 * W), BF16),
                pltpu.VMEM((CZ, 2, G, TR, 2 * W), F32),
                pltpu.VMEM((G, 2, 2, TR, W), F32),
                pltpu.VMEM((G, 2, 2, TR, W), F32),
                pltpu.SMEM((2, G), jnp.int32),
                dma,
                dma((2, NC)),
                dma((2, NC)),
                dma((2, 3)),
                dma((2, 3)),
                dma((G,)),
                dma((G,)),
            ],
            compiler_params=pltpu.CompilerParams(collective_id=0, has_side_effects=True),
        )(live_slices, shear_slopes, palette, depth_order, tile_owner, density)
        return out[:, :, None]

    placed = (P(depth_axis, row_axis, None), P(), P(), P(), P(), P())
    return jax.shard_map(
        body,
        mesh=mesh,
        in_specs=placed,
        out_specs=P(None, None, depth_axis, row_axis, None),
        check_vma=False,
    )
```

```python
import functools

import jax
import jax.numpy as jnp
from jax import lax
from jax.experimental import pallas as pl
from jax.experimental.pallas import tpu as pltpu
from jax.sharding import PartitionSpec as P

LIGHT = (0.48, 0.6, 0.64)
LOG2E = 1.4426950408889634
CHUNKS = ((0, 32), (32, 64), (64, 96), (96, 128))
F32, BF16 = jnp.float32, jnp.bfloat16


def spread(first, second, inside):
    return jnp.where(inside, jnp.where((first - second <= 4) & (second - first <= 4), 1.0, 0.0), 0.0)


def kernel(
    G, R, depth_axis, row_axis,
    live_ref, slopes_ref, palette_ref, order_ref, owner_ref, dens_ref,
    out_ref,
    ext, summed, rowed, smooth, dcol, band, layers, shear, sheared, outbox, inbox, inverse,
    local_sem, zsend, zrecv, rsend, rrecv, tsend, trecv,
):
    me = lax.axis_index(depth_axis)
    col = lax.axis_index(row_axis)
    CZ, CY, W = dens_ref.shape
    TR = CY // G
    NC = len(CHUNKS)
    has = {-1: me > 0, 1: me < G - 1}
    hasr = {-1: col > 0, 1: col < R - 1}
    at = lambda g, r: {depth_axis: g, row_axis: r}

    barrier = pltpu.get_barrier_semaphore()

    def greet(k, carry):
        pl.semaphore_signal(barrier, inc=1, device_id=at(lax.rem(me + k, G), col))
        return carry

    lax.fori_loop(1, G, greet, 0)
    for dr in (-1, 1):
        for dz in (-1, 0, 1):
            ok = hasr[dr] if dz == 0 else hasr[dr] & has[dz]

            @pl.when(ok)
            def _():
                pl.semaphore_signal(barrier, inc=1, device_id=at(me + dz, col + dr))

    local = pltpu.make_async_copy(dens_ref, ext.at[5:13, 8:136, :], local_sem)
    local.start()
    beside = hasr[-1].astype(jnp.int32) + hasr[1].astype(jnp.int32)
    above = has[-1].astype(jnp.int32) + has[1].astype(jnp.int32)
    pl.semaphore_wait(barrier, (G - 1) + beside * (1 + above))

    def zcopy(dz, k):
        lo, hi = CHUNKS[k]
        src = dens_ref.at[3:8, lo:hi, :] if dz == 1 else dens_ref.at[0:5, lo:hi, :]
        dst = ext.at[0:5, 8 + lo : 8 + hi, :] if dz == 1 else ext.at[13:18, 8 + lo : 8 + hi, :]
        side = (dz + 1) // 2
        return pltpu.make_async_remote_copy(
            src, dst, zsend.at[side, k], zrecv.at[side, k], device_id=at(me + dz, col)
        )

    def rcopy(dz, dr):
        zs, zd = {0: (slice(0, 8), slice(5, 13)), 1: (slice(3, 8), slice(0, 5)), -1: (slice(0, 5), slice(13, 18))}[dz]
        rs, rd = {1: (slice(120, 128), slice(0, 8)), -1: (slice(0, 8), slice(136, 144))}[dr]
        side = (dr + 1) // 2
        return pltpu.make_async_remote_copy(
            dens_ref.at[zs, rs, :], ext.at[zd, rd, :], rsend.at[side, dz + 1], rrecv.at[side, dz + 1],
            device_id=at(me + dz, col + dr),
        )

    zcopies = [(dz, k) for k in range(NC) for dz in (1, -1)]
    rcopies = [(dz, dr) for dr in (-1, 1) for dz in (1, -1, 0)]

    def allowed(dz, dr):
        return hasr[dr] if dz == 0 else hasr[dr] & has[dz]

    for dz in (1, -1):
        @pl.when(has[dz])
        def _():
            zcopy(dz, 0).start()
    for dz, dr in rcopies:
        @pl.when(allowed(dz, dr))
        def _():
            rcopy(dz, dr).start()
    for dz in (1, -1):
        @pl.when(has[dz])
        def _():
            for k in range(1, NC):
                zcopy(dz, k).start()

    for dz in (1, -1):
        @pl.when(jnp.logical_not(has[-dz]))
        def _():
            zd = slice(0, 5) if dz == 1 else slice(13, 18)
            ext[zd, :, :] = jnp.zeros((5, CY + 16, W), F32)
    for dr in (1, -1):
        @pl.when(jnp.logical_not(hasr[-dr]))
        def _():
            rd = slice(0, 8) if dr == 1 else slice(136, 144)
            ext[:, rd, :] = jnp.zeros((CZ + 10, 8, W), F32)

    def invert(d, carry):
        for v in range(2):
            found = jnp.int32(0)
            for t in range(G):
                found = jnp.maximum(found, t * (owner_ref[v, t] == d).astype(jnp.int32))
            inverse[v, d] = found
        return carry

    lax.fori_loop(0, G, invert, 0)

    source = lax.broadcasted_iota(jnp.int32, (W, W), 0)
    target = lax.broadcasted_iota(jnp.int32, (W, W), 1)
    ones = spread(source, target, True)
    diff = spread(source, target + 1, target + 1 < W) - spread(source, target - 1, target >= 1)
    for half in range(2):
        band[half * W : half * W + W, 0:W] = ones.astype(BF16)
        band[half * W : half * W + W, W : 2 * W] = diff.astype(BF16)

    offset = (source - target).astype(F32)

    def shears(z, carry):
        depth = (me * CZ + z).astype(F32) + (0.5 - 0.5 * CZ * G)
        for v in range(2):
            m = jnp.maximum(0.0, 1.0 - jnp.abs(offset + slopes_ref[v] * depth))
            shear[z, :, v * W : v * W + W] = m.astype(BF16)
        return carry

    lax.fori_loop(0, CZ, shears, 0)

    live = live_ref[me, col]
    brightest = jnp.maximum(jnp.maximum(palette_ref[0], palette_ref[1]), palette_ref[2])

    def depth_sums(lo, hi):
        def block(b, carry):
            rows = pl.ds(pl.multiple_of(lo + 8 * b, 8), 8)
            x = [ext[z, rows, :] for z in range(CZ + 10)]
            two = [x[i] + x[i + 1] for i in range(CZ + 8)]
            four = [two[i] + two[i + 2] for i in range(CZ + 6)]
            eight = [four[i] + four[i + 4] for i in range(CZ + 2)]
            for z in range(CZ + 2):
                summed[z, rows, :] = eight[z] + x[z + 8]
            return carry

        lax.fori_loop(0, (hi - lo) // 8, block, 0)

    def smooth_rows(lo, hi):
        def layer(z, carry):
            for j in range(lo, hi, 8):
                s = [summed[z, j + k : j + 8 + k, :] for k in range(9)]
                rowed[z, j : j + 8, :] = (
                    ((s[0] + s[1]) + (s[2] + s[3])) + ((s[4] + s[5]) + (s[6] + s[7])) + s[8]
                )
            return carry

        lax.fori_loop(0, CZ + 2, layer, 0)

    def smooth_cols(lo, hi):
        n = (CZ + 2) * (hi - lo)
        x = rowed[:, lo:hi, :].reshape(n, W)
        high = x.astype(BF16)
        low = (x - high.astype(F32)).astype(BF16)
        both = jnp.dot(
            jnp.concatenate([high, low], axis=1), band[...], preferred_element_type=F32
        )
        smooth[:, lo:hi, :] = both[:, 0:W].reshape(CZ + 2, hi - lo, W)
        dcol[:, lo:hi, :] = both[:, W : 2 * W].reshape(CZ + 2, hi - lo, W)

    def shade(lo, hi):
        def layer(z, carry):
            alive = (z < live).astype(jnp.int32).astype(F32)
            bright_of = alive * brightest
            for r in range(lo, hi, 16):
                q = r + 4
                n = 16
                center = smooth[z + 1, q : q + n, :]
                dz = smooth[z + 2, q : q + n, :] - smooth[z, q : q + n, :]
                dr = smooth[z + 1, q + 1 : q + n + 1, :] - smooth[z + 1, q - 1 : q + n - 1, :]
                dc = dcol[z + 1, q : q + n, :]
                along = jnp.maximum(0.0, LIGHT[0] * dz + LIGHT[1] * dr + LIGHT[2] * dc)
                facing = along * lax.rsqrt(dz * dz + dr * dr + dc * dc + 0.01 * 1458.0 * 1458.0)
                y = center * (2.0 / 729.0)
                soft = jnp.maximum(y, 0.0) + jnp.log(1.0 + jnp.exp(-jnp.abs(y)))
                opacity = 1.0 - jnp.exp(soft * (-3.0 / (CZ * G)))
                layers[z, 0, r : r + n, :] = (opacity * (0.25 + 0.75 * facing) * bright_of).astype(BF16)
                layers[z, 1, r : r + n, :] = (opacity * alive).astype(BF16)
            return carry

        lax.fori_loop(0, CZ, layer, 0)

    def shear_rows(lo, hi):
        for z in range(CZ):
            lhs = layers[z, :, lo:hi, :].reshape(2 * (hi - lo), W)
            out = jnp.dot(lhs, shear[z], preferred_element_type=F32)
            sheared[z, :, lo // TR : hi // TR] = out.reshape(2, (hi - lo) // TR, TR, 2 * W)

    def clear(lo, hi):
        for dz in (-1, 1):
            @pl.when(jnp.logical_not(has[dz]))
            def _():
                smooth[0 if dz == -1 else CZ + 1, lo:hi, :] = jnp.zeros((hi - lo, W), F32)

    local.wait()
    for dz, dr in rcopies:
        @pl.when(allowed(-dz, -dr))
        def _():
            rcopy(dz, dr).wait_recv()

    depth_sums(0, 8)
    depth_sums(CY + 8, CY + 16)
    done_rows, done_smooth = 0, 0
    for k in range(NC):
        for dz in (1, -1):
            @pl.when(has[-dz])
            def _():
                zcopy(dz, k).wait_recv()
        lo, hi = CHUNKS[k]
        depth_sums(8 + lo, 8 + hi)
        last = k == NC - 1
        upto = CY + 8 if last else hi
        smooth_rows(done_smooth, upto)
        smooth_cols(done_smooth, upto)
        clear(done_smooth, upto)
        if k == 0:
            @pl.when(jnp.logical_not(hasr[-1]))
            def _():
                smooth[:, 0:4, :] = jnp.zeros((CZ + 2, 4, W), F32)
        if last:
            @pl.when(jnp.logical_not(hasr[1]))
            def _():
                smooth[:, CY + 4 : CY + 8, :] = jnp.zeros((CZ + 2, 4, W), F32)
        done_smooth = upto
        shaded = CY if last else hi - 16
        shade(done_rows, shaded)
        shear_rows(done_rows, shaded)
        done_rows = shaded

    def tcopy(d):
        return pltpu.make_async_remote_copy(
            outbox.at[d], inbox.at[me], tsend.at[d], trecv.at[me], device_id=at(d, col)
        )

    def march(d, box, slot):
        for v in range(2):
            tile = inverse[v, d]
            shaded, transmit = None, None
            for z in range(CZ) if v == 0 else range(CZ - 1, -1, -1):
                b = sheared[z, 0, tile, :, v * W : v * W + W]
                a = sheared[z, 1, tile, :, v * W : v * W + W]
                shaded = b if shaded is None else shaded + transmit * b
                transmit = 1.0 - a if transmit is None else transmit * (1.0 - a)
            box[slot, v, 0] = shaded
            box[slot, v, 1] = transmit

    def send(k, carry):
        d = lax.rem(me + k, G)
        march(d, outbox, d)
        tcopy(d).start()
        return carry

    lax.fori_loop(1, G, send, 0)
    march(me, inbox, me)

    def receive(k, carry):
        s = lax.rem(me + G - k, G)
        pltpu.make_async_remote_copy(
            outbox.at[s], inbox.at[s], tsend.at[s], trecv.at[s], device_id=at(s, col)
        ).wait_recv()
        return carry

    lax.fori_loop(1, G, receive, 0)

    for v in range(2):
        def blend(i, carry):
            shaded, transmit = carry
            s = order_ref[v, i]
            return shaded + transmit * inbox[s, v, 0], transmit * inbox[s, v, 1]

        shaded, transmit = lax.fori_loop(
            0, G, blend, (jnp.zeros((TR, W), F32), jnp.ones((TR, W), F32)), unroll=True
        )
        for c in range(3):
            out_ref[v, c] = shaded * (palette_ref[c] / brightest)
        out_ref[v, 3] = 1.0 - transmit

    for dz in (1, -1):
        @pl.when(has[dz])
        def _():
            for k in range(NC):
                zcopy(dz, k).wait_send()
    for dz, dr in rcopies:
        @pl.when(allowed(dz, dr))
        def _():
            rcopy(dz, dr).wait_send()

    def sent(k, carry):
        d = lax.rem(me + k, G)
        tcopy(d).wait_send()
        return carry

    lax.fori_loop(1, G, sent, 0)


def solution(mesh):
    depth_axis, row_axis = mesh.axis_names
    G, R = mesh.shape[depth_axis], mesh.shape[row_axis]

    def body(density, live_slices, shear_slopes, palette, depth_order, tile_owner):
        CZ, CY, W = density.shape
        TR = CY // G
        smem = pl.BlockSpec(memory_space=pltpu.SMEM)
        dma = pltpu.SemaphoreType.DMA
        NC = len(CHUNKS)
        out = pl.pallas_call(
            functools.partial(kernel, G, R, depth_axis, row_axis),
            out_shape=jax.ShapeDtypeStruct((2, 4, TR, W), F32),
            in_specs=[smem] * 5 + [pl.BlockSpec(memory_space=pl.ANY)],
            out_specs=pl.BlockSpec(memory_space=pltpu.VMEM),
            scratch_shapes=[
                pltpu.VMEM((CZ + 10, CY + 16, W), F32),
                pltpu.VMEM((CZ + 2, CY + 16, W), F32),
                pltpu.VMEM((CZ + 2, CY + 8, W), F32),
                pltpu.VMEM((CZ + 2, CY + 8, W), F32),
                pltpu.VMEM((CZ + 2, CY + 8, W), F32),
                pltpu.VMEM((2 * W, 2 * W), BF16),
                pltpu.VMEM((CZ, 2, CY, W), BF16),
                pltpu.VMEM((CZ, W, 2 * W), BF16),
                pltpu.VMEM((CZ, 2, G, TR, 2 * W), F32),
                pltpu.VMEM((G, 2, 2, TR, W), F32),
                pltpu.VMEM((G, 2, 2, TR, W), F32),
                pltpu.SMEM((2, G), jnp.int32),
                dma,
                dma((2, NC)),
                dma((2, NC)),
                dma((2, 3)),
                dma((2, 3)),
                dma((G,)),
                dma((G,)),
            ],
            compiler_params=pltpu.CompilerParams(collective_id=0, has_side_effects=True),
        )(live_slices, shear_slopes, palette, depth_order, tile_owner, density)
        return out[:, :, None]

    placed = (P(depth_axis, row_axis, None), P(), P(), P(), P(), P())
    return jax.shard_map(
        body,
        mesh=mesh,
        in_specs=placed,
        out_specs=P(None, None, depth_axis, row_axis, None),
        check_vma=False,
    )
```

```python
import functools

import jax
import jax.numpy as jnp
from jax import lax
from jax.experimental import pallas as pl
from jax.experimental.pallas import tpu as pltpu
from jax.sharding import PartitionSpec as P

LIGHT = (0.48, 0.6, 0.64)
LOG2E = 1.4426950408889634
CHUNKS = ((0, 32), (32, 64), (64, 96), (96, 128))
F32, BF16 = jnp.float32, jnp.bfloat16


def spread(first, second, inside):
    return jnp.where(inside, jnp.where((first - second <= 4) & (second - first <= 4), 1.0, 0.0), 0.0)


def kernel(
    G, R, depth_axis, row_axis,
    live_ref, slopes_ref, palette_ref, order_ref, owner_ref, dens_ref,
    out_ref,
    ext, summed, rowed, smooth, dcol, band, layers, shear, sheared, outbox, inbox, inverse,
    local_sem, zsend, zrecv, rsend, rrecv, tsend, trecv, known,
):
    me = lax.axis_index(depth_axis)
    col = lax.axis_index(row_axis)
    CZ, CY, W = dens_ref.shape
    TR = CY // G
    NC = len(CHUNKS)
    has = {-1: me > 0, 1: me < G - 1}
    hasr = {-1: col > 0, 1: col < R - 1}
    at = lambda g, r: {depth_axis: g, row_axis: r}

    barrier = pltpu.get_barrier_semaphore()

    def ring(k):
        return at(lax.rem(me + (k + G), G), col)

    for k in (-1, 1):
        pl.semaphore_signal(barrier, inc=1, device_id=ring(k))
    for dr in (-1, 1):
        for dz in (-1, 0, 1):
            ok = hasr[dr] if dz == 0 else hasr[dr] & has[dz]

            @pl.when(ok)
            def _():
                pl.semaphore_signal(barrier, inc=1, device_id=at(me + dz, col + dr))

    local = pltpu.make_async_copy(dens_ref, ext.at[5:13, 8:136, :], local_sem)
    local.start()
    beside = hasr[-1].astype(jnp.int32) + hasr[1].astype(jnp.int32)
    above = has[-1].astype(jnp.int32) + has[1].astype(jnp.int32)
    pl.semaphore_wait(barrier, 2 + beside * (1 + above))

    rounds = [1 << j for j in range((G // 4).bit_length())]

    def tell(j):
        for side, sign in enumerate((1, -1)):
            pl.semaphore_signal(known.at[j, side], inc=1, device_id=ring(sign * rounds[j]))

    def hear(j):
        for side in range(2):
            pl.semaphore_wait(known.at[j, side], 1)

    def zcopy(dz, k):
        lo, hi = CHUNKS[k]
        src = dens_ref.at[3:8, lo:hi, :] if dz == 1 else dens_ref.at[0:5, lo:hi, :]
        dst = ext.at[0:5, 8 + lo : 8 + hi, :] if dz == 1 else ext.at[13:18, 8 + lo : 8 + hi, :]
        side = (dz + 1) // 2
        return pltpu.make_async_remote_copy(
            src, dst, zsend.at[side, k], zrecv.at[side, k], device_id=at(me + dz, col)
        )

    def rcopy(dz, dr):
        zs, zd = {0: (slice(0, 8), slice(5, 13)), 1: (slice(3, 8), slice(0, 5)), -1: (slice(0, 5), slice(13, 18))}[dz]
        rs, rd = {1: (slice(120, 128), slice(0, 8)), -1: (slice(0, 8), slice(136, 144))}[dr]
        side = (dr + 1) // 2
        return pltpu.make_async_remote_copy(
            dens_ref.at[zs, rs, :], ext.at[zd, rd, :], rsend.at[side, dz + 1], rrecv.at[side, dz + 1],
            device_id=at(me + dz, col + dr),
        )

    zcopies = [(dz, k) for k in range(NC) for dz in (1, -1)]
    rcopies = [(dz, dr) for dr in (-1, 1) for dz in (1, -1, 0)]

    def allowed(dz, dr):
        return hasr[dr] if dz == 0 else hasr[dr] & has[dz]

    for dz in (1, -1):
        @pl.when(has[dz])
        def _():
            zcopy(dz, 0).start()
    for dz, dr in rcopies:
        @pl.when(allowed(dz, dr))
        def _():
            rcopy(dz, dr).start()
    for dz in (1, -1):
        @pl.when(has[dz])
        def _():
            for k in range(1, NC):
                zcopy(dz, k).start()

    tell(0)

    for dz in (1, -1):
        @pl.when(jnp.logical_not(has[-dz]))
        def _():
            zd = slice(0, 5) if dz == 1 else slice(13, 18)
            ext[zd, :, :] = jnp.zeros((5, CY + 16, W), F32)
    for dr in (1, -1):
        @pl.when(jnp.logical_not(hasr[-dr]))
        def _():
            rd = slice(0, 8) if dr == 1 else slice(136, 144)
            ext[:, rd, :] = jnp.zeros((CZ + 10, 8, W), F32)

    def invert(d, carry):
        for v in range(2):
            found = jnp.int32(0)
            for t in range(G):
                found = jnp.maximum(found, t * (owner_ref[v, t] == d).astype(jnp.int32))
            inverse[v, d] = found
        return carry

    lax.fori_loop(0, G, invert, 0)

    source = lax.broadcasted_iota(jnp.int32, (W, W), 0)
    target = lax.broadcasted_iota(jnp.int32, (W, W), 1)
    ones = spread(source, target, True)
    diff = spread(source, target + 1, target + 1 < W) - spread(source, target - 1, target >= 1)
    for half in range(2):
        band[half * W : half * W + W, 0:W] = ones.astype(BF16)
        band[half * W : half * W + W, W : 2 * W] = diff.astype(BF16)

    offset = (source - target).astype(F32)

    def shears(z, carry):
        depth = (me * CZ + z).astype(F32) + (0.5 - 0.5 * CZ * G)
        for v in range(2):
            m = jnp.maximum(0.0, 1.0 - jnp.abs(offset + slopes_ref[v] * depth))
            shear[z, :, v * W : v * W + W] = m.astype(BF16)
        return carry

    lax.fori_loop(0, CZ, shears, 0)

    live = live_ref[me, col]
    brightest = jnp.maximum(jnp.maximum(palette_ref[0], palette_ref[1]), palette_ref[2])

    def depth_sums(lo, hi):
        def block(b, carry):
            rows = pl.ds(pl.multiple_of(lo + 8 * b, 8), 8)
            x = [ext[z, rows, :] for z in range(CZ + 10)]
            two = [x[i] + x[i + 1] for i in range(CZ + 8)]
            four = [two[i] + two[i + 2] for i in range(CZ + 6)]
            eight = [four[i] + four[i + 4] for i in range(CZ + 2)]
            for z in range(CZ + 2):
                summed[z, rows, :] = eight[z] + x[z + 8]
            return carry

        lax.fori_loop(0, (hi - lo) // 8, block, 0)

    def smooth_rows(lo, hi):
        def layer(z, carry):
            for j in range(lo, hi, 8):
                s = [summed[z, j + k : j + 8 + k, :] for k in range(9)]
                rowed[z, j : j + 8, :] = (
                    ((s[0] + s[1]) + (s[2] + s[3])) + ((s[4] + s[5]) + (s[6] + s[7])) + s[8]
                )
            return carry

        lax.fori_loop(0, CZ + 2, layer, 0)

    def smooth_cols(lo, hi):
        n = (CZ + 2) * (hi - lo)
        x = rowed[:, lo:hi, :].reshape(n, W)
        high = x.astype(BF16)
        low = (x - high.astype(F32)).astype(BF16)
        both = jnp.dot(
            jnp.concatenate([high, low], axis=1), band[...], preferred_element_type=F32
        )
        smooth[:, lo:hi, :] = both[:, 0:W].reshape(CZ + 2, hi - lo, W)
        dcol[:, lo:hi, :] = both[:, W : 2 * W].reshape(CZ + 2, hi - lo, W)

    def shade(lo, hi):
        def layer(z, carry):
            alive = (z < live).astype(jnp.int32).astype(F32)
            bright_of = alive * brightest
            for r in range(lo, hi, 16):
                q = r + 4
                n = 16
                center = smooth[z + 1, q : q + n, :]
                dz = smooth[z + 2, q : q + n, :] - smooth[z, q : q + n, :]
                dr = smooth[z + 1, q + 1 : q + n + 1, :] - smooth[z + 1, q - 1 : q + n - 1, :]
                dc = dcol[z + 1, q : q + n, :]
                along = jnp.maximum(0.0, LIGHT[0] * dz + LIGHT[1] * dr + LIGHT[2] * dc)
                facing = along * lax.rsqrt(dz * dz + dr * dr + dc * dc + 0.01 * 1458.0 * 1458.0)
                y = center * (2.0 / 729.0)
                soft = jnp.maximum(y, 0.0) + jnp.log(1.0 + jnp.exp(-jnp.abs(y)))
                opacity = 1.0 - jnp.exp(soft * (-3.0 / (CZ * G)))
                layers[z, 0, r : r + n, :] = (opacity * (0.25 + 0.75 * facing) * bright_of).astype(BF16)
                layers[z, 1, r : r + n, :] = (opacity * alive).astype(BF16)
            return carry

        lax.fori_loop(0, CZ, layer, 0)

    def shear_rows(lo, hi):
        for z in range(CZ):
            lhs = layers[z, :, lo:hi, :].reshape(2 * (hi - lo), W)
            out = jnp.dot(lhs, shear[z], preferred_element_type=F32)
            sheared[z, :, lo // TR : hi // TR] = out.reshape(2, (hi - lo) // TR, TR, 2 * W)

    def clear(lo, hi):
        for dz in (-1, 1):
            @pl.when(jnp.logical_not(has[dz]))
            def _():
                smooth[0 if dz == -1 else CZ + 1, lo:hi, :] = jnp.zeros((hi - lo, W), F32)

    hear(0)
    if len(rounds) > 1:
        tell(1)
    local.wait()
    for dz, dr in rcopies:
        @pl.when(allowed(-dz, -dr))
        def _():
            rcopy(dz, dr).wait_recv()

    depth_sums(0, 8)
    depth_sums(CY + 8, CY + 16)
    done_rows, done_smooth = 0, 0
    for k in range(NC):
        for dz in (1, -1):
            @pl.when(has[-dz])
            def _():
                zcopy(dz, k).wait_recv()
        lo, hi = CHUNKS[k]
        depth_sums(8 + lo, 8 + hi)
        last = k == NC - 1
        upto = CY + 8 if last else hi
        smooth_rows(done_smooth, upto)
        smooth_cols(done_smooth, upto)
        clear(done_smooth, upto)
        if k == 0:
            @pl.when(jnp.logical_not(hasr[-1]))
            def _():
                smooth[:, 0:4, :] = jnp.zeros((CZ + 2, 4, W), F32)
        if last:
            @pl.when(jnp.logical_not(hasr[1]))
            def _():
                smooth[:, CY + 4 : CY + 8, :] = jnp.zeros((CZ + 2, 4, W), F32)
        done_smooth = upto
        shaded = CY if last else hi - 16
        shade(done_rows, shaded)
        shear_rows(done_rows, shaded)
        done_rows = shaded
        if k + 1 < len(rounds):
            hear(k + 1)
            if k + 2 < len(rounds):
                tell(k + 2)

    def tcopy(d):
        return pltpu.make_async_remote_copy(
            outbox.at[d], inbox.at[me], tsend.at[d], trecv.at[me], device_id=at(d, col)
        )

    def coded(x):
        return (jnp.sqrt(jnp.minimum(x, 1.0)) * 65535.0 + 0.5).astype(jnp.int32)

    full = 1.0625 * brightest
    per_full = 1.0 / full

    def march(d, box, slot):
        for v in range(2):
            tile = inverse[v, d]
            shaded, transmit = None, None
            for z in range(CZ) if v == 0 else range(CZ - 1, -1, -1):
                b = sheared[z, 0, tile, :, v * W : v * W + W]
                a = sheared[z, 1, tile, :, v * W : v * W + W]
                shaded = b if shaded is None else shaded + transmit * b
                transmit = 1.0 - a if transmit is None else transmit * (1.0 - a)
            box[slot, v] = (coded(shaded * per_full) << 16) | coded(1.0 - transmit)

    def peer(i):
        j = i // 2
        chip = lax.rem(me // 2 + G // 4 + (j + 1) // 2 * (1 - 2 * lax.rem(j, 2)) + G // 2, G // 2)
        return 2 * chip + lax.rem(i + me, 2)

    other = me + 1 - 2 * lax.rem(me, 2)

    def send(i, carry):
        d = peer(i)
        march(d, outbox, d)
        tcopy(d).start()
        return carry

    lax.fori_loop(0, G - 2, send, 0)
    march(other, outbox, other)
    tcopy(other).start()
    march(me, inbox, me)

    def receive(k, carry):
        s = lax.rem(me + G - k, G)
        pltpu.make_async_remote_copy(
            outbox.at[s], inbox.at[s], tsend.at[s], trecv.at[s], device_id=at(s, col)
        ).wait_recv()
        return carry

    lax.fori_loop(1, G, receive, 0)

    for v in range(2):
        def blend(i, carry):
            shaded, transmit = carry
            s = order_ref[v, i]
            word = inbox[s, v]
            c = ((word >> 16) & 65535).astype(F32) * (1.0 / 65535.0)
            a = (word & 65535).astype(F32) * (1.0 / 65535.0)
            return shaded + transmit * (c * c), transmit * (1.0 - a * a)

        shaded, transmit = lax.fori_loop(
            0, G, blend, (jnp.zeros((TR, W), F32), jnp.ones((TR, W), F32)), unroll=True
        )
        for c in range(3):
            out_ref[v, c] = shaded * (palette_ref[c] * 1.0625)
        out_ref[v, 3] = 1.0 - transmit

    for dz in (1, -1):
        @pl.when(has[dz])
        def _():
            for k in range(NC):
                zcopy(dz, k).wait_send()
    for dz, dr in rcopies:
        @pl.when(allowed(dz, dr))
        def _():
            rcopy(dz, dr).wait_send()

    def sent(k, carry):
        d = lax.rem(me + k, G)
        tcopy(d).wait_send()
        return carry

    lax.fori_loop(1, G, sent, 0)


def solution(mesh):
    depth_axis, row_axis = mesh.axis_names
    G, R = mesh.shape[depth_axis], mesh.shape[row_axis]

    def body(density, live_slices, shear_slopes, palette, depth_order, tile_owner):
        CZ, CY, W = density.shape
        TR = CY // G
        smem = pl.BlockSpec(memory_space=pltpu.SMEM)
        dma = pltpu.SemaphoreType.DMA
        NC = len(CHUNKS)
        out = pl.pallas_call(
            functools.partial(kernel, G, R, depth_axis, row_axis),
            out_shape=jax.ShapeDtypeStruct((2, 4, TR, W), F32),
            in_specs=[smem] * 5 + [pl.BlockSpec(memory_space=pl.ANY)],
            out_specs=pl.BlockSpec(memory_space=pltpu.VMEM),
            scratch_shapes=[
                pltpu.VMEM((CZ + 10, CY + 16, W), F32),
                pltpu.VMEM((CZ + 2, CY + 16, W), F32),
                pltpu.VMEM((CZ + 2, CY + 8, W), F32),
                pltpu.VMEM((CZ + 2, CY + 8, W), F32),
                pltpu.VMEM((CZ + 2, CY + 8, W), F32),
                pltpu.VMEM((2 * W, 2 * W), BF16),
                pltpu.VMEM((CZ, 2, CY, W), BF16),
                pltpu.VMEM((CZ, W, 2 * W), BF16),
                pltpu.VMEM((CZ, 2, G, TR, 2 * W), F32),
                pltpu.VMEM((G, 2, TR, W), jnp.int32),
                pltpu.VMEM((G, 2, TR, W), jnp.int32),
                pltpu.SMEM((2, G), jnp.int32),
                dma,
                dma((2, NC)),
                dma((2, NC)),
                dma((2, 3)),
                dma((2, 3)),
                dma((G,)),
                dma((G,)),
                pltpu.SemaphoreType.REGULAR((3, 2)),
            ],
            compiler_params=pltpu.CompilerParams(collective_id=0, has_side_effects=True),
        )(live_slices, shear_slopes, palette, depth_order, tile_owner, density)
        return out[:, :, None]

    placed = (P(depth_axis, row_axis, None), P(), P(), P(), P(), P())
    return jax.shard_map(
        body,
        mesh=mesh,
        in_specs=placed,
        out_specs=P(None, None, depth_axis, row_axis, None),
        check_vma=False,
    )
```

```python
import functools

import jax
import jax.numpy as jnp
from jax import lax
from jax.experimental import pallas as pl
from jax.experimental.pallas import tpu as pltpu
from jax.sharding import PartitionSpec as P

LIGHT = (0.48, 0.6, 0.64)
LOG2E = 1.4426950408889634
CHUNKS = ((0, 32), (32, 64), (64, 96), (96, 128))
F32, BF16 = jnp.float32, jnp.bfloat16


def spread(first, second, inside):
    return jnp.where(inside, jnp.where((first - second <= 4) & (second - first <= 4), 1.0, 0.0), 0.0)


def kernel(
    G, R, depth_axis, row_axis,
    live_ref, slopes_ref, palette_ref, order_ref, owner_ref, dens_ref,
    out_ref,
    ext, summed, rowed, smooth, dcol, band, layers, shear, sheared, outbox, inbox, inverse,
    local_sem, zsend, zrecv, rsend, rrecv, tsend, trecv, known,
):
    me = lax.axis_index(depth_axis)
    col = lax.axis_index(row_axis)
    CZ, CY, W = dens_ref.shape
    TR = CY // G
    NC = len(CHUNKS)
    has = {-1: me > 0, 1: me < G - 1}
    hasr = {-1: col > 0, 1: col < R - 1}
    at = lambda g, r: {depth_axis: g, row_axis: r}

    barrier = pltpu.get_barrier_semaphore()

    def ring(k):
        return at(lax.rem(me + (k + G), G), col)

    for k in (-1, 1):
        pl.semaphore_signal(barrier, inc=1, device_id=ring(k))
    for dr in (-1, 1):
        for dz in (-1, 0, 1):
            ok = hasr[dr] if dz == 0 else hasr[dr] & has[dz]

            @pl.when(ok)
            def _():
                pl.semaphore_signal(barrier, inc=1, device_id=at(me + dz, col + dr))

    local = pltpu.make_async_copy(dens_ref, ext.at[5:13, 8:136, :], local_sem)
    local.start()
    beside = hasr[-1].astype(jnp.int32) + hasr[1].astype(jnp.int32)
    above = has[-1].astype(jnp.int32) + has[1].astype(jnp.int32)
    pl.semaphore_wait(barrier, 2 + beside * (1 + above))

    rounds = [1 << j for j in range((G // 4).bit_length())]

    def tell(j):
        for side, sign in enumerate((1, -1)):
            pl.semaphore_signal(known.at[j, side], inc=1, device_id=ring(sign * rounds[j]))

    def hear(j):
        for side in range(2):
            pl.semaphore_wait(known.at[j, side], 1)

    def zcopy(dz, k):
        lo, hi = CHUNKS[k]
        src = dens_ref.at[3:8, lo:hi, :] if dz == 1 else dens_ref.at[0:5, lo:hi, :]
        dst = ext.at[0:5, 8 + lo : 8 + hi, :] if dz == 1 else ext.at[13:18, 8 + lo : 8 + hi, :]
        side = (dz + 1) // 2
        return pltpu.make_async_remote_copy(
            src, dst, zsend.at[side, k], zrecv.at[side, k], device_id=at(me + dz, col)
        )

    def rcopy(dz, dr):
        zs, zd = {0: (slice(0, 8), slice(5, 13)), 1: (slice(3, 8), slice(0, 5)), -1: (slice(0, 5), slice(13, 18))}[dz]
        rs, rd = {1: (slice(120, 128), slice(0, 8)), -1: (slice(0, 8), slice(136, 144))}[dr]
        side = (dr + 1) // 2
        return pltpu.make_async_remote_copy(
            dens_ref.at[zs, rs, :], ext.at[zd, rd, :], rsend.at[side, dz + 1], rrecv.at[side, dz + 1],
            device_id=at(me + dz, col + dr),
        )

    zcopies = [(dz, k) for k in range(NC) for dz in (1, -1)]
    rcopies = [(dz, dr) for dr in (-1, 1) for dz in (1, -1, 0)]

    def allowed(dz, dr):
        return hasr[dr] if dz == 0 else hasr[dr] & has[dz]

    for dz in (1, -1):
        @pl.when(has[dz])
        def _():
            zcopy(dz, 0).start()
    for dz, dr in rcopies:
        @pl.when(allowed(dz, dr))
        def _():
            rcopy(dz, dr).start()
    for dz in (1, -1):
        @pl.when(has[dz])
        def _():
            for k in range(1, NC):
                zcopy(dz, k).start()

    tell(0)

    for dz in (1, -1):
        @pl.when(jnp.logical_not(has[-dz]))
        def _():
            zd = slice(0, 5) if dz == 1 else slice(13, 18)
            ext[zd, :, :] = jnp.zeros((5, CY + 16, W), F32)
    for dr in (1, -1):
        @pl.when(jnp.logical_not(hasr[-dr]))
        def _():
            rd = slice(0, 8) if dr == 1 else slice(136, 144)
            ext[:, rd, :] = jnp.zeros((CZ + 10, 8, W), F32)

    def invert(d, carry):
        for v in range(2):
            found = jnp.int32(0)
            for t in range(G):
                found = jnp.maximum(found, t * (owner_ref[v, t] == d).astype(jnp.int32))
            inverse[v, d] = found
        return carry

    lax.fori_loop(0, G, invert, 0)

    source = lax.broadcasted_iota(jnp.int32, (W, W), 0)
    target = lax.broadcasted_iota(jnp.int32, (W, W), 1)
    ones = spread(source, target, True)
    diff = spread(source, target + 1, target + 1 < W) - spread(source, target - 1, target >= 1)
    for half in range(2):
        band[half * W : half * W + W, 0:W] = ones.astype(BF16)
        band[half * W : half * W + W, W : 2 * W] = diff.astype(BF16)

    offset = (source - target).astype(F32)

    def shears(z, carry):
        depth = (me * CZ + z).astype(F32) + (0.5 - 0.5 * CZ * G)
        for v in range(2):
            m = jnp.maximum(0.0, 1.0 - jnp.abs(offset + slopes_ref[v] * depth))
            shear[z, :, v * W : v * W + W] = m.astype(BF16)
        return carry

    lax.fori_loop(0, CZ, shears, 0)

    live = live_ref[me, col]
    brightest = jnp.maximum(jnp.maximum(palette_ref[0], palette_ref[1]), palette_ref[2])

    ambient = 0.25 * brightest
    light = [0.75 * part * brightest for part in LIGHT]
    rate = -3.0 * LOG2E / (CZ * G)

    def depth_sums(lo, hi):
        def block(b, carry):
            rows = pl.ds(pl.multiple_of(lo + 8 * b, 8), 8)
            x = [ext[z, rows, :] for z in range(CZ + 10)]
            two = [x[i] + x[i + 1] for i in range(CZ + 8)]
            four = [two[i] + two[i + 2] for i in range(CZ + 6)]
            eight = [four[i] + four[i + 4] for i in range(CZ + 2)]
            for z in range(CZ + 2):
                summed[z, rows, :] = eight[z] + x[z + 8]
            return carry

        n = (hi - lo) // 8
        lax.fori_loop(0, n, block, 0, unroll=True)

    def smooth_rows(lo, hi):
        def layer(z, carry):
            for j in range(lo, hi, 8):
                s = [summed[z, j + k : j + 8 + k, :] for k in range(9)]
                rowed[z, j : j + 8, :] = (
                    ((s[0] + s[1]) + (s[2] + s[3])) + ((s[4] + s[5]) + (s[6] + s[7])) + s[8]
                )
            return carry

        lax.fori_loop(0, CZ + 2, layer, 0, unroll=True)

    def smooth_cols(lo, hi):
        n = (CZ + 2) * (hi - lo)
        x = rowed[:, lo:hi, :].reshape(n, W)
        high = x.astype(BF16)
        low = (x - high.astype(F32)).astype(BF16)
        both = jnp.dot(
            jnp.concatenate([high, low], axis=1), band[...], preferred_element_type=F32
        )
        smooth[:, lo:hi, :] = both[:, 0:W].reshape(CZ + 2, hi - lo, W)
        dcol[:, lo:hi, :] = both[:, W : 2 * W].reshape(CZ + 2, hi - lo, W)

    def shade(lo, hi):
        def layer(z, carry):
            fade = rate * (z < live).astype(jnp.int32).astype(F32)
            for r in range(lo, hi, 16):
                q = r + 4
                n = 16
                center = smooth[z + 1, q : q + n, :]
                dz = smooth[z + 2, q : q + n, :] - smooth[z, q : q + n, :]
                dr = smooth[z + 1, q + 1 : q + n + 1, :] - smooth[z + 1, q - 1 : q + n - 1, :]
                dc = dcol[z + 1, q : q + n, :]
                along = jnp.maximum(0.0, light[0] * dz + light[1] * dr + light[2] * dc)
                lit = ambient + along * lax.rsqrt((dz * dz + 0.01 * 1458.0 * 1458.0) + (dr * dr + dc * dc))
                soft = jnp.maximum(center * (2.0 / 729.0), 0.0) + jnp.log(
                    1.0 + jnp.exp2(jnp.abs(center) * (-2.0 * LOG2E / 729.0))
                )
                opacity = 1.0 - jnp.exp2(soft * fade)
                layers[z, 0, r : r + n, :] = (opacity * lit).astype(BF16)
                layers[z, 1, r : r + n, :] = opacity.astype(BF16)
            return carry

        lax.fori_loop(0, CZ, layer, 0, unroll=True)

    def shear_rows(lo, hi):
        for z in range(CZ):
            lhs = layers[z, :, lo:hi, :].reshape(2 * (hi - lo), W)
            out = jnp.dot(lhs, shear[z], preferred_element_type=F32)
            sheared[z, :, lo // TR : hi // TR] = out.reshape(2, (hi - lo) // TR, TR, 2 * W)

    def clear(lo, hi):
        for dz in (-1, 1):
            @pl.when(jnp.logical_not(has[dz]))
            def _():
                smooth[0 if dz == -1 else CZ + 1, lo:hi, :] = jnp.zeros((hi - lo, W), F32)

    hear(0)
    if len(rounds) > 1:
        tell(1)
    local.wait()
    for dz, dr in rcopies:
        @pl.when(allowed(-dz, -dr))
        def _():
            rcopy(dz, dr).wait_recv()

    depth_sums(0, 8)
    depth_sums(CY + 8, CY + 16)
    done_rows, done_smooth = 0, 0
    pending = None
    for k in range(NC):
        for dz in (1, -1):
            @pl.when(has[-dz])
            def _():
                zcopy(dz, k).wait_recv()
        lo, hi = CHUNKS[k]
        depth_sums(8 + lo, 8 + hi)
        last = k == NC - 1
        upto = CY + 8 if last else hi
        smooth_rows(done_smooth, upto)
        if pending is not None:
            shear_rows(*pending)
        smooth_cols(done_smooth, upto)
        clear(done_smooth, upto)
        if k == 0:
            @pl.when(jnp.logical_not(hasr[-1]))
            def _():
                smooth[:, 0:4, :] = jnp.zeros((CZ + 2, 4, W), F32)
        if last:
            @pl.when(jnp.logical_not(hasr[1]))
            def _():
                smooth[:, CY + 4 : CY + 8, :] = jnp.zeros((CZ + 2, 4, W), F32)
        done_smooth = upto
        shaded = CY if last else hi - 16
        shade(done_rows, shaded)
        pending = (done_rows, shaded)
        done_rows = shaded
        if k + 1 < len(rounds):
            hear(k + 1)
            if k + 2 < len(rounds):
                tell(k + 2)

    shear_rows(*pending)

    def tcopy(d):
        return pltpu.make_async_remote_copy(
            outbox.at[d], inbox.at[me], tsend, trecv, device_id=at(d, col)
        )

    def coded(x):
        return (jnp.sqrt(jnp.minimum(x, 1.0)) * 65535.0 + 0.5).astype(jnp.int32)

    full = 1.0625 * brightest
    per_full = 1.0 / full

    def march(d, box, slot):
        for v in range(2):
            tile = inverse[v, d]
            shaded, transmit = None, None
            for z in range(CZ) if v == 0 else range(CZ - 1, -1, -1):
                b = sheared[z, 0, tile, :, v * W : v * W + W]
                a = sheared[z, 1, tile, :, v * W : v * W + W]
                shaded = b if shaded is None else shaded + transmit * b
                transmit = 1.0 - a if transmit is None else transmit * (1.0 - a)
            box[slot, v] = (coded(shaded * per_full) << 16) | coded(1.0 - transmit)

    def peer(i):
        j = i // 2
        chip = lax.rem(me // 2 + G // 4 + (j + 1) // 2 * (1 - 2 * lax.rem(j, 2)) + G // 2, G // 2)
        return 2 * chip + lax.rem(i + me, 2)

    other = me + 1 - 2 * lax.rem(me, 2)

    def send(i, carry):
        d = peer(i)
        march(d, outbox, d)
        tcopy(d).start()
        return carry

    lax.fori_loop(0, G - 2, send, 0, unroll=2)
    march(other, outbox, other)
    tcopy(other).start()
    march(me, inbox, me)

    others = pltpu.make_async_remote_copy(
        outbox.at[0 : G - 1], inbox.at[0 : G - 1], tsend, trecv, device_id=at(other, col)
    )
    others.wait_recv()

    for v in range(2):
        def blend(i, carry):
            shaded, transmit = carry
            s = order_ref[v, i]
            word = inbox[s, v]
            c = ((word >> 16) & 65535).astype(F32) * (1.0 / 65535.0)
            a = (word & 65535).astype(F32) * (1.0 / 65535.0)
            return shaded + transmit * (c * c), transmit * (1.0 - a * a)

        shaded, transmit = lax.fori_loop(
            0, G, blend, (jnp.zeros((TR, W), F32), jnp.ones((TR, W), F32)), unroll=True
        )
        for c in range(3):
            out_ref[v, c] = shaded * (palette_ref[c] * 1.0625)
        out_ref[v, 3] = 1.0 - transmit

    for dz in (1, -1):
        @pl.when(has[dz])
        def _():
            for k in range(NC):
                zcopy(dz, k).wait_send()
    for dz, dr in rcopies:
        @pl.when(allowed(dz, dr))
        def _():
            rcopy(dz, dr).wait_send()

    others.wait_send()


def solution(mesh):
    depth_axis, row_axis = mesh.axis_names
    G, R = mesh.shape[depth_axis], mesh.shape[row_axis]

    def body(density, live_slices, shear_slopes, palette, depth_order, tile_owner):
        CZ, CY, W = density.shape
        TR = CY // G
        smem = pl.BlockSpec(memory_space=pltpu.SMEM)
        dma = pltpu.SemaphoreType.DMA
        NC = len(CHUNKS)
        out = pl.pallas_call(
            functools.partial(kernel, G, R, depth_axis, row_axis),
            out_shape=jax.ShapeDtypeStruct((2, 4, TR, W), F32),
            in_specs=[smem] * 5 + [pl.BlockSpec(memory_space=pl.ANY)],
            out_specs=pl.BlockSpec(memory_space=pltpu.VMEM),
            scratch_shapes=[
                pltpu.VMEM((CZ + 10, CY + 16, W), F32),
                pltpu.VMEM((CZ + 2, CY + 16, W), F32),
                pltpu.VMEM((CZ + 2, CY + 8, W), F32),
                pltpu.VMEM((CZ + 2, CY + 8, W), F32),
                pltpu.VMEM((CZ + 2, CY + 8, W), F32),
                pltpu.VMEM((2 * W, 2 * W), BF16),
                pltpu.VMEM((CZ, 2, CY, W), BF16),
                pltpu.VMEM((CZ, W, 2 * W), BF16),
                pltpu.VMEM((CZ, 2, G, TR, 2 * W), F32),
                pltpu.VMEM((G, 2, TR, W), jnp.int32),
                pltpu.VMEM((G, 2, TR, W), jnp.int32),
                pltpu.SMEM((2, G), jnp.int32),
                dma,
                dma((2, NC)),
                dma((2, NC)),
                dma((2, 3)),
                dma((2, 3)),
                dma,
                dma,
                pltpu.SemaphoreType.REGULAR((3, 2)),
            ],
            compiler_params=pltpu.CompilerParams(collective_id=0, has_side_effects=True),
        )(live_slices, shear_slopes, palette, depth_order, tile_owner, density)
        return out[:, :, None]

    placed = (P(depth_axis, row_axis, None), P(), P(), P(), P(), P())
    return jax.shard_map(
        body,
        mesh=mesh,
        in_specs=placed,
        out_specs=P(None, None, depth_axis, row_axis, None),
        check_vma=False,
    )
```

```python
import functools

import jax
import jax.numpy as jnp
from jax import lax
from jax.experimental import pallas as pl
from jax.experimental.pallas import tpu as pltpu
from jax.sharding import PartitionSpec as P

LIGHT = (0.48, 0.6, 0.64)
LOG2E = 1.4426950408889634
CHUNKS = ((0, 48), (48, 80), (80, 112), (112, 128))
WORK = (
    {"rows": ((8, 48),), "shade": ((16, 32),)},
    {"rows": ((48, 80),), "shade": ((32, 64),)},
    {"rows": ((80, 112), (0, 8)), "shade": ((64, 96), (0, 16))},
    {"rows": ((112, 136),), "shade": ((96, 128),)},
)
F32, BF16 = jnp.float32, jnp.bfloat16


def spread(first, second, inside):
    return jnp.where(inside, jnp.where((first - second <= 4) & (second - first <= 4), 1.0, 0.0), 0.0)


def kernel(
    G, R, depth_axis, row_axis,
    live_hbm, slopes_hbm, palette_hbm, order_hbm, owner_hbm, dens_ref,
    out_ref,
    ext, summed, rowed, smooth, dcol, band, layers, shear, sheared, outbox, inbox, inverse,
    live_ref, slopes_ref, palette_ref, order_ref, owner_ref, table_sem, local_sem, zsend, zrecv, rsend, rrecv, tsend, trecv, known,
):
    me = lax.axis_index(depth_axis)
    col = lax.axis_index(row_axis)
    CZ, CY, W = dens_ref.shape
    TR = CY // G
    NC = len(CHUNKS)
    has = {-1: me > 0, 1: me < G - 1}
    hasr = {-1: col > 0, 1: col < R - 1}
    at = lambda g, r: {depth_axis: g, row_axis: r}

    barrier = pltpu.get_barrier_semaphore()

    def ring(k):
        return at(lax.rem(me + (k + G), G), col)

    for k in (-1, 1):
        pl.semaphore_signal(barrier, inc=1, device_id=ring(k))
    for dr in (-1, 1):
        for dz in (-1, 0, 1):
            ok = hasr[dr] if dz == 0 else hasr[dr] & has[dz]

            @pl.when(ok)
            def _():
                pl.semaphore_signal(barrier, inc=1, device_id=at(me + dz, col + dr))

    tables = [
        pltpu.make_async_copy(a, b, table_sem.at[i])
        for i, (a, b) in enumerate(
            (
                (owner_hbm, owner_ref), (slopes_hbm, slopes_ref), (live_hbm, live_ref),
                (palette_hbm, palette_ref), (order_hbm, order_ref),
            )
        )
    ]
    for table in tables:
        table.start()
    local = pltpu.make_async_copy(dens_ref, ext.at[5:13, 8:136, :], local_sem)
    local.start()
    beside = hasr[-1].astype(jnp.int32) + hasr[1].astype(jnp.int32)
    above = has[-1].astype(jnp.int32) + has[1].astype(jnp.int32)
    pl.semaphore_wait(barrier, 2 + beside * (1 + above))

    rounds = [1 << j for j in range((G // 4).bit_length())]

    def tell(j):
        for side, sign in enumerate((1, -1)):
            pl.semaphore_signal(known.at[j, side], inc=1, device_id=ring(sign * rounds[j]))

    def hear(j):
        for side in range(2):
            pl.semaphore_wait(known.at[j, side], 1)

    def zcopy(dz, k):
        lo, hi = CHUNKS[k]
        src = dens_ref.at[3:8, lo:hi, :] if dz == 1 else dens_ref.at[0:5, lo:hi, :]
        dst = ext.at[0:5, 8 + lo : 8 + hi, :] if dz == 1 else ext.at[13:18, 8 + lo : 8 + hi, :]
        side = (dz + 1) // 2
        return pltpu.make_async_remote_copy(
            src, dst, zsend.at[side, k], zrecv.at[side, k], device_id=at(me + dz, col)
        )

    def rcopy(dz, dr):
        zs, zd = {0: (slice(0, 8), slice(5, 13)), 1: (slice(3, 8), slice(0, 5)), -1: (slice(0, 5), slice(13, 18))}[dz]
        rs, rd = {1: (slice(120, 128), slice(0, 8)), -1: (slice(0, 8), slice(136, 144))}[dr]
        side = (dr + 1) // 2
        return pltpu.make_async_remote_copy(
            dens_ref.at[zs, rs, :], ext.at[zd, rd, :], rsend.at[side, dz + 1], rrecv.at[side, dz + 1],
            device_id=at(me + dz, col + dr),
        )

    zcopies = [(dz, k) for k in range(NC) for dz in (1, -1)]
    rcopies = [(dz, dr) for dr in (-1, 1) for dz in (1, -1, 0)]

    def allowed(dz, dr):
        return hasr[dr] if dz == 0 else hasr[dr] & has[dz]

    for dz in (1, -1):
        @pl.when(has[dz])
        def _():
            zcopy(dz, 0).start()
    for dz, dr in rcopies:
        @pl.when(allowed(dz, dr))
        def _():
            rcopy(dz, dr).start()
    for dz in (1, -1):
        @pl.when(has[dz])
        def _():
            for k in range(1, NC):
                zcopy(dz, k).start()

    tell(0)

    for dz in (1, -1):
        @pl.when(jnp.logical_not(has[-dz]))
        def _():
            zd = slice(0, 5) if dz == 1 else slice(13, 18)
            ext[zd, :, :] = jnp.zeros((5, CY + 16, W), F32)
    for dr in (1, -1):
        @pl.when(jnp.logical_not(hasr[-dr]))
        def _():
            rd = slice(0, 8) if dr == 1 else slice(136, 144)
            ext[:, rd, :] = jnp.zeros((CZ + 10, 8, W), F32)

    for table in tables:
        table.wait()

    def invert(d, carry):
        for v in range(2):
            found = jnp.int32(0)
            for t in range(G):
                found = jnp.maximum(found, t * (owner_ref[v, t] == d).astype(jnp.int32))
            inverse[v, d] = found
        return carry

    lax.fori_loop(0, G, invert, 0)

    source = lax.broadcasted_iota(jnp.int32, (W, W), 0)
    target = lax.broadcasted_iota(jnp.int32, (W, W), 1)
    ones = spread(source, target, True)
    diff = spread(source, target + 1, target + 1 < W) - spread(source, target - 1, target >= 1)
    for half in range(2):
        band[half * W : half * W + W, 0:W] = ones.astype(BF16)
        band[half * W : half * W + W, W : 2 * W] = diff.astype(BF16)

    offset = (source - target).astype(F32)

    def shears(z, carry):
        depth = (me * CZ + z).astype(F32) + (0.5 - 0.5 * CZ * G)
        for v in range(2):
            m = jnp.maximum(0.0, 1.0 - jnp.abs(offset + slopes_ref[v] * depth))
            shear[z, :, v * W : v * W + W] = m.astype(BF16)
        return carry

    lax.fori_loop(0, CZ, shears, 0)

    live = live_ref[me, col]
    brightest = jnp.maximum(jnp.maximum(palette_ref[0], palette_ref[1]), palette_ref[2])

    ambient = 0.25 * brightest
    light = [0.75 * part * brightest for part in LIGHT]
    rate = -3.0 * LOG2E / (CZ * G)

    def depth_sums(lo, hi):
        def block(b, carry):
            rows = pl.ds(pl.multiple_of(lo + 8 * b, 8), 8)
            x = [ext[z, rows, :] for z in range(CZ + 10)]
            two = [x[i] + x[i + 1] for i in range(CZ + 8)]
            four = [two[i] + two[i + 2] for i in range(CZ + 6)]
            eight = [four[i] + four[i + 4] for i in range(CZ + 2)]
            for z in range(CZ + 2):
                summed[z, rows, :] = eight[z] + x[z + 8]
            return carry

        n = (hi - lo) // 8
        lax.fori_loop(0, n, block, 0, unroll=True)

    def smooth_rows(lo, hi):
        def layer(z, carry):
            for j in range(lo, hi, 8):
                s = [summed[z, j + k : j + 8 + k, :] for k in range(9)]
                rowed[z, j : j + 8, :] = (
                    ((s[0] + s[1]) + (s[2] + s[3])) + ((s[4] + s[5]) + (s[6] + s[7])) + s[8]
                )
            return carry

        lax.fori_loop(0, CZ + 2, layer, 0, unroll=True)

    def smooth_cols(lo, hi):
        n = (CZ + 2) * (hi - lo)
        x = rowed[:, lo:hi, :].reshape(n, W)
        high = x.astype(BF16)
        low = (x - high.astype(F32)).astype(BF16)
        both = jnp.dot(
            jnp.concatenate([high, low], axis=1), band[...], preferred_element_type=F32
        )
        smooth[:, lo:hi, :] = both[:, 0:W].reshape(CZ + 2, hi - lo, W)
        dcol[:, lo:hi, :] = both[:, W : 2 * W].reshape(CZ + 2, hi - lo, W)

    def shade(lo, hi):
        def layer(z, carry):
            fade = rate * (z < live).astype(jnp.int32).astype(F32)
            for r in range(lo, hi, 16):
                q = r + 4
                n = 16
                center = smooth[z + 1, q : q + n, :]
                dz = smooth[z + 2, q : q + n, :] - smooth[z, q : q + n, :]
                dr = smooth[z + 1, q + 1 : q + n + 1, :] - smooth[z + 1, q - 1 : q + n - 1, :]
                dc = dcol[z + 1, q : q + n, :]
                along = jnp.maximum(0.0, light[0] * dz + light[1] * dr + light[2] * dc)
                lit = ambient + along * lax.rsqrt((dz * dz + 0.01 * 1458.0 * 1458.0) + (dr * dr + dc * dc))
                soft = jnp.maximum(center * (2.0 / 729.0), 0.0) + jnp.log(
                    1.0 + jnp.exp2(jnp.abs(center) * (-2.0 * LOG2E / 729.0))
                )
                opacity = 1.0 - jnp.exp2(soft * fade)
                layers[z, 0, r : r + n, :] = (opacity * lit).astype(BF16)
                layers[z, 1, r : r + n, :] = opacity.astype(BF16)
            return carry

        lax.fori_loop(0, CZ, layer, 0, unroll=True)

    def shear_rows(lo, hi):
        for z in range(CZ):
            lhs = layers[z, :, lo:hi, :].reshape(2 * (hi - lo), W)
            out = jnp.dot(lhs, shear[z], preferred_element_type=F32)
            sheared[z, :, lo // TR : hi // TR] = out.reshape(2, (hi - lo) // TR, TR, 2 * W)

    def clear(lo, hi):
        for dz in (-1, 1):
            @pl.when(jnp.logical_not(has[dz]))
            def _():
                smooth[0 if dz == -1 else CZ + 1, lo:hi, :] = jnp.zeros((hi - lo, W), F32)

    hear(0)
    if len(rounds) > 1:
        tell(1)
    local.wait()
    def sides_in(dr):
        for dz in (1, -1, 0):
            @pl.when(allowed(-dz, -dr))
            def _():
                rcopy(dz, dr).wait_recv()

    pending = []
    for k, ((lo, hi), ranges) in enumerate(zip(CHUNKS, WORK)):
        for dz in (1, -1):
            @pl.when(has[-dz])
            def _():
                zcopy(dz, k).wait_recv()
        depth_sums(8 + lo, 8 + hi)
        if ranges["rows"][-1][0] == 0:
            sides_in(1)
            depth_sums(0, 8)
        if ranges["rows"][-1][1] == CY + 8:
            sides_in(-1)
            depth_sums(CY + 8, CY + 16)
        for first, end in ranges["rows"]:
            smooth_rows(first, end)
        for job in pending:
            shear_rows(*job)
        for first, end in ranges["rows"]:
            smooth_cols(first, end)
            clear(first, end)
            if first == 0:
                @pl.when(jnp.logical_not(hasr[-1]))
                def _():
                    smooth[:, 0:4, :] = jnp.zeros((CZ + 2, 4, W), F32)
            if end == CY + 8:
                @pl.when(jnp.logical_not(hasr[1]))
                def _():
                    smooth[:, CY + 4 : CY + 8, :] = jnp.zeros((CZ + 2, 4, W), F32)
        for job in ranges["shade"]:
            shade(*job)
        pending = ranges["shade"]
        if k + 1 < len(rounds):
            hear(k + 1)
            if k + 2 < len(rounds):
                tell(k + 2)

    for job in pending:
        shear_rows(*job)

    def tcopy(d):
        return pltpu.make_async_remote_copy(
            outbox.at[d], inbox.at[me], tsend, trecv, device_id=at(d, col)
        )

    def coded(x):
        return (jnp.sqrt(jnp.minimum(x, 1.0)) * 65535.0 + 0.5).astype(jnp.int32)

    full = 1.0625 * brightest
    per_full = 1.0 / full

    def march(d, box, slot):
        for v in range(2):
            tile = inverse[v, d]
            shaded, transmit = None, None
            for z in range(CZ) if v == 0 else range(CZ - 1, -1, -1):
                b = sheared[z, 0, tile, :, v * W : v * W + W]
                a = sheared[z, 1, tile, :, v * W : v * W + W]
                shaded = b if shaded is None else shaded + transmit * b
                transmit = 1.0 - a if transmit is None else transmit * (1.0 - a)
            box[slot, v] = (coded(shaded * per_full) << 16) | coded(1.0 - transmit)

    other = me + 1 - 2 * (me & 1)
    for i in range(G - 2):
        j = i // 2
        away = G // 4 + (j + 1) // 2 * (1 - 2 * (j % 2))
        d = 2 * ((me // 2 + away) & (G // 2 - 1)) + ((i + me) & 1)
        march(d, outbox, d)
        tcopy(d).start()
    march(other, outbox, other)
    tcopy(other).start()
    march(me, inbox, me)

    others = pltpu.make_async_remote_copy(
        outbox.at[0 : G - 1], inbox.at[0 : G - 1], tsend, trecv, device_id=at(other, col)
    )
    for dz in (1, -1):
        @pl.when(has[dz])
        def _():
            for k in range(NC):
                zcopy(dz, k).wait_send()
    for dz, dr in rcopies:
        @pl.when(allowed(dz, dr))
        def _():
            rcopy(dz, dr).wait_send()
    others.wait_send()
    others.wait_recv()

    for v in range(2):
        def blend(i, carry):
            shaded, transmit = carry
            s = order_ref[v, i]
            word = inbox[s, v]
            c = ((word >> 16) & 65535).astype(F32) * (1.0 / 65535.0)
            a = (word & 65535).astype(F32) * (1.0 / 65535.0)
            return shaded + transmit * (c * c), transmit * (1.0 - a * a)

        shaded, transmit = lax.fori_loop(
            0, G, blend, (jnp.zeros((TR, W), F32), jnp.ones((TR, W), F32)), unroll=True
        )
        for c in range(3):
            out_ref[v, c] = shaded * (palette_ref[c] * 1.0625)
        out_ref[v, 3] = 1.0 - transmit


def solution(mesh):
    depth_axis, row_axis = mesh.axis_names
    G, R = mesh.shape[depth_axis], mesh.shape[row_axis]

    def body(density, live_slices, shear_slopes, palette, depth_order, tile_owner):
        CZ, CY, W = density.shape
        TR = CY // G
        arrays = (live_slices, shear_slopes, palette, depth_order, tile_owner, density)
        dma = pltpu.SemaphoreType.DMA
        NC = len(CHUNKS)
        out = pl.pallas_call(
            functools.partial(kernel, G, R, depth_axis, row_axis),
            out_shape=jax.ShapeDtypeStruct((2, 4, TR, W), F32),
            in_specs=[pl.BlockSpec(memory_space=pl.ANY)] * 6,
            out_specs=pl.BlockSpec(memory_space=pltpu.VMEM),
            scratch_shapes=[
                pltpu.VMEM((CZ + 10, CY + 16, W), F32),
                pltpu.VMEM((CZ + 2, CY + 16, W), F32),
                pltpu.VMEM((CZ + 2, CY + 8, W), F32),
                pltpu.VMEM((CZ + 2, CY + 8, W), F32),
                pltpu.VMEM((CZ + 2, CY + 8, W), F32),
                pltpu.VMEM((2 * W, 2 * W), BF16),
                pltpu.VMEM((CZ, 2, CY, W), BF16),
                pltpu.VMEM((CZ, W, 2 * W), BF16),
                pltpu.VMEM((CZ, 2, G, TR, 2 * W), F32),
                pltpu.VMEM((G, 2, TR, W), jnp.int32),
                pltpu.VMEM((G, 2, TR, W), jnp.int32),
                pltpu.SMEM((2, G), jnp.int32),
                *(pltpu.SMEM(a.shape, a.dtype) for a in arrays[:5]),
                dma((5,)),
                dma,
                dma((2, NC)),
                dma((2, NC)),
                dma((2, 3)),
                dma((2, 3)),
                dma,
                dma,
                pltpu.SemaphoreType.REGULAR((3, 2)),
            ],
            compiler_params=pltpu.CompilerParams(collective_id=0, has_side_effects=True, vmem_limit_bytes=12 << 20),
        )(*(pltpu.with_memory_space_constraint(a, pltpu.HBM) for a in arrays))
        return out[:, :, None]

    placed = (P(depth_axis, row_axis, None), P(), P(), P(), P(), P())
    return jax.shard_map(
        body,
        mesh=mesh,
        in_specs=placed,
        out_specs=P(None, None, depth_axis, row_axis, None),
        check_vma=False,
    )
```

```python
import functools

import jax
import jax.numpy as jnp
from jax import lax
from jax.experimental import pallas as pl
from jax.experimental.pallas import tpu as pltpu
from jax.sharding import PartitionSpec as P

LIGHT = (0.48, 0.6, 0.64)
LOG2E = 1.4426950408889634
STEPS = 32767.0 / 96.0
CHUNKS = ((0, 32), (32, 80), (80, 128))
WORK = (
    {"rows": ((8, 32),), "shade": ()},
    {"rows": ((32, 80), (0, 8)), "shade": ((16, 64), (0, 16))},
    {"rows": ((80, 136),), "shade": ((64, 128),)},
)
F32, BF16 = jnp.float32, jnp.bfloat16


def spread(first, second, inside):
    return jnp.where(inside, jnp.where((first - second <= 4) & (second - first <= 4), 1.0, 0.0), 0.0)


def kernel(
    G, R, depth_axis, row_axis,
    live_hbm, slopes_hbm, palette_hbm, order_hbm, owner_hbm, dens_ref,
    out_ref,
    raw, quant, codes, halo, side_rows, summed, rowed, smooth, dcol, band, layers, shear, sheared, outbox, inbox, inverse,
    live_ref, slopes_ref, palette_ref, order_ref, owner_ref, table_sem, local_sem, zsend, zrecv, rsend, rrecv, tsend, trecv, known,
):
    me = lax.axis_index(depth_axis)
    col = lax.axis_index(row_axis)
    CZ, CY, W = dens_ref.shape
    TR = CY // G
    NC = len(CHUNKS)
    has = {-1: me > 0, 1: me < G - 1}
    hasr = {-1: col > 0, 1: col < R - 1}
    at = lambda g, r: {depth_axis: g, row_axis: r}

    barrier = pltpu.get_barrier_semaphore()

    def ring(k):
        return at(lax.rem(me + (k + G), G), col)

    for k in (-1, 1):
        pl.semaphore_signal(barrier, inc=1, device_id=ring(k))
    for dr in (-1, 1):
        for dz in (-1, 0, 1):
            ok = hasr[dr] if dz == 0 else hasr[dr] & has[dz]

            @pl.when(ok)
            def _():
                pl.semaphore_signal(barrier, inc=1, device_id=at(me + dz, col + dr))

    tables = [
        pltpu.make_async_copy(a, b, table_sem.at[i])
        for i, (a, b) in enumerate(
            (
                (owner_hbm, owner_ref), (slopes_hbm, slopes_ref), (live_hbm, live_ref),
                (palette_hbm, palette_ref), (order_hbm, order_ref),
            )
        )
    ]
    for table in tables:
        table.start()
    local = [
        pltpu.make_async_copy(dens_ref.at[:, lo:hi, :], raw.at[:, lo:hi, :], local_sem.at[k])
        for k, (lo, hi) in enumerate(CHUNKS)
    ]
    for part in local:
        part.start()

    def encode(k):
        lo, hi = CHUNKS[k]
        half = (hi - lo) // 2
        local[k].wait()
        for z in range(CZ):
            x = jnp.round(raw[z, lo:hi, :] * STEPS)
            quant[z, lo:hi, :] = x
            i = x.astype(jnp.int32)
            codes[z, lo // 2 : hi // 2, :] = (i[:half] << 16) + (i[half:] + 32768)

    encode(0)
    beside = hasr[-1].astype(jnp.int32) + hasr[1].astype(jnp.int32)
    above = has[-1].astype(jnp.int32) + has[1].astype(jnp.int32)
    pl.semaphore_wait(barrier, 2 + beside * (1 + above))

    rounds = [1 << j for j in range((G // 4).bit_length())]

    def tell(j):
        for side, sign in enumerate((1, -1)):
            pl.semaphore_signal(known.at[j, side], inc=1, device_id=ring(sign * rounds[j]))

    def hear(j):
        for side in range(2):
            pl.semaphore_wait(known.at[j, side], 1)

    def zcopy(dz, k):
        rows = slice(CHUNKS[k][0] // 2, CHUNKS[k][1] // 2)
        src = codes.at[3:8, rows, :] if dz == 1 else codes.at[0:5, rows, :]
        dst = halo.at[(1 - dz) // 2, :, rows, :]
        side = (dz + 1) // 2
        return pltpu.make_async_remote_copy(
            src, dst, zsend.at[side, k], zrecv.at[side, k], device_id=at(me + dz, col)
        )

    def rcopy(dz, dr):
        zs, zd = {0: (slice(0, 8), slice(5, 13)), 1: (slice(3, 8), slice(0, 5)), -1: (slice(0, 5), slice(13, 18))}[dz]
        rs, rd = {1: (slice(120, 128), 0), -1: (slice(0, 8), 1)}[dr]
        side = (dr + 1) // 2
        return pltpu.make_async_remote_copy(
            dens_ref.at[zs, rs, :], side_rows.at[rd, zd], rsend.at[side, dz + 1], rrecv.at[side, dz + 1],
            device_id=at(me + dz, col + dr),
        )

    zcopies = [(dz, k) for k in range(NC) for dz in (1, -1)]
    rcopies = [(dz, dr) for dr in (-1, 1) for dz in (1, -1, 0)]

    def allowed(dz, dr):
        return hasr[dr] if dz == 0 else hasr[dr] & has[dz]

    for dz in (1, -1):
        @pl.when(has[dz])
        def _():
            zcopy(dz, 0).start()
    for dz, dr in rcopies:
        @pl.when(allowed(dz, dr))
        def _():
            rcopy(dz, dr).start()
    for k in range(1, NC):
        encode(k)
        for dz in (1, -1):
            @pl.when(has[dz])
            def _():
                zcopy(dz, k).start()

    tell(0)

    for dz in (1, -1):
        @pl.when(jnp.logical_not(has[-dz]))
        def _():
            halo[(1 - dz) // 2] = jnp.full((5, CY // 2, W), 32768, jnp.int32)
            zd = slice(0, 5) if dz == 1 else slice(13, 18)
            side_rows[:, zd] = jnp.zeros((2, 5, 8, W), F32)
    for dr in (1, -1):
        @pl.when(jnp.logical_not(hasr[-dr]))
        def _():
            side_rows[(1 - dr) // 2] = jnp.zeros((CZ + 10, 8, W), F32)

    for table in tables:
        table.wait()

    def invert(d, carry):
        for v in range(2):
            found = jnp.int32(0)
            for t in range(G):
                found = jnp.maximum(found, t * (owner_ref[v, t] == d).astype(jnp.int32))
            inverse[v, d] = found
        return carry

    lax.fori_loop(0, G, invert, 0)

    source = lax.broadcasted_iota(jnp.int32, (W, W), 0)
    target = lax.broadcasted_iota(jnp.int32, (W, W), 1)
    ones = spread(source, target, True)
    diff = spread(source, target + 1, target + 1 < W) - spread(source, target - 1, target >= 1)
    for half in range(2):
        band[half * W : half * W + W, 0:W] = ones.astype(BF16)
        band[half * W : half * W + W, W : 2 * W] = diff.astype(BF16)

    offset = (source - target).astype(F32)

    def shears(z, carry):
        depth = (me * CZ + z).astype(F32) + (0.5 - 0.5 * CZ * G)
        for v in range(2):
            m = jnp.maximum(0.0, 1.0 - jnp.abs(offset + slopes_ref[v] * depth))
            shear[z, :, v * W : v * W + W] = m.astype(BF16)
        return carry

    lax.fori_loop(0, CZ, shears, 0)

    live = live_ref[me, col]
    brightest = jnp.maximum(jnp.maximum(palette_ref[0], palette_ref[1]), palette_ref[2])

    ambient = 0.25 * brightest
    light = [0.75 * part * brightest for part in LIGHT]
    rate = -3.0 * LOG2E / (CZ * G)

    def depth_sum(x, q):
        two = [x[i] + x[i + 1] for i in range(CZ + 8)]
        four = [two[i] + two[i + 2] for i in range(CZ + 6)]
        eight = [four[i] + four[i + 4] for i in range(CZ + 2)]
        for z in range(CZ + 2):
            summed[z, q : q + 8, :] = eight[z] + x[z + 8]

    def depth_sums(k):
        lo, hi = CHUNKS[k]
        half = (hi - lo) // 2
        for b in range(0, half, 8):
            words = [[halo[side, z, lo // 2 + b : lo // 2 + b + 8, :] for z in range(5)] for side in range(2)]
            for part in range(2):
                r = lo + part * half + b
                below, above = [
                    [((w >> 16) if part == 0 else (w & 65535) - 32768).astype(F32) for w in ws] for ws in words
                ]
                depth_sum(below + [quant[z, r : r + 8, :] for z in range(CZ)] + above, r + 8)

    def side_sums(side):
        x = [jnp.round(side_rows[side, z] * STEPS) for z in range(CZ + 10)]
        depth_sum(x, side * (CY + 8))

    def smooth_rows(lo, hi):
        def layer(z, carry):
            for j in range(lo, hi, 8):
                s = [summed[z, j + k : j + 8 + k, :] for k in range(9)]
                rowed[z, j : j + 8, :] = (
                    ((s[0] + s[1]) + (s[2] + s[3])) + ((s[4] + s[5]) + (s[6] + s[7])) + s[8]
                )
            return carry

        lax.fori_loop(0, CZ + 2, layer, 0, unroll=True)

    def smooth_cols(lo, hi):
        n = (CZ + 2) * (hi - lo)
        x = rowed[:, lo:hi, :].reshape(n, W)
        high = x.astype(BF16)
        low = (x - high.astype(F32)).astype(BF16)
        both = jnp.dot(
            jnp.concatenate([high, low], axis=1), band[...], preferred_element_type=F32
        )
        smooth[:, lo:hi, :] = both[:, 0:W].reshape(CZ + 2, hi - lo, W)
        dcol[:, lo:hi, :] = both[:, W : 2 * W].reshape(CZ + 2, hi - lo, W)

    def shade(lo, hi):
        def layer(z, carry):
            fade = rate * (z < live).astype(jnp.int32).astype(F32)
            for r in range(lo, hi, 16):
                q = r + 4
                n = 16
                center = smooth[z + 1, q : q + n, :]
                dz = smooth[z + 2, q : q + n, :] - smooth[z, q : q + n, :]
                dr = smooth[z + 1, q + 1 : q + n + 1, :] - smooth[z + 1, q - 1 : q + n - 1, :]
                dc = dcol[z + 1, q : q + n, :]
                along = jnp.maximum(0.0, light[0] * dz + light[1] * dr + light[2] * dc)
                lit = ambient + along * lax.rsqrt((dz * dz + 0.01 * (1458.0 * STEPS) ** 2) + (dr * dr + dc * dc))
                soft = jnp.maximum(center * (2.0 / (729.0 * STEPS)), 0.0) + jnp.log(
                    1.0 + jnp.exp2(jnp.abs(center) * (-2.0 * LOG2E / (729.0 * STEPS)))
                )
                opacity = 1.0 - jnp.exp2(soft * fade)
                layers[z, 0, r : r + n, :] = (opacity * lit).astype(BF16)
                layers[z, 1, r : r + n, :] = opacity.astype(BF16)
            return carry

        lax.fori_loop(0, CZ, layer, 0, unroll=True)

    def shear_rows(lo, hi):
        for z in range(CZ):
            lhs = layers[z, :, lo:hi, :].reshape(2 * (hi - lo), W)
            out = jnp.dot(lhs, shear[z], preferred_element_type=F32)
            sheared[z, :, lo // TR : hi // TR] = out.reshape(2, (hi - lo) // TR, TR, 2 * W)

    def clear(lo, hi):
        for dz in (-1, 1):
            @pl.when(jnp.logical_not(has[dz]))
            def _():
                smooth[0 if dz == -1 else CZ + 1, lo:hi, :] = jnp.zeros((hi - lo, W), F32)

    hear(0)
    if len(rounds) > 1:
        tell(1)
    def sides_in(dr):
        for dz in (1, -1, 0):
            @pl.when(allowed(-dz, -dr))
            def _():
                rcopy(dz, dr).wait_recv()

    pending = []
    for k, ranges in enumerate(WORK):
        for dz in (1, -1):
            @pl.when(has[-dz])
            def _():
                zcopy(dz, k).wait_recv()
        depth_sums(k)
        if ranges["rows"][-1][0] == 0:
            sides_in(1)
            side_sums(0)
        if ranges["rows"][-1][1] == CY + 8:
            sides_in(-1)
            side_sums(1)
        for first, end in ranges["rows"]:
            smooth_rows(first, end)
        for job in pending:
            shear_rows(*job)
        for first, end in ranges["rows"]:
            smooth_cols(first, end)
            clear(first, end)
            if first == 0:
                @pl.when(jnp.logical_not(hasr[-1]))
                def _():
                    smooth[:, 0:4, :] = jnp.zeros((CZ + 2, 4, W), F32)
            if end == CY + 8:
                @pl.when(jnp.logical_not(hasr[1]))
                def _():
                    smooth[:, CY + 4 : CY + 8, :] = jnp.zeros((CZ + 2, 4, W), F32)
        for job in ranges["shade"]:
            shade(*job)
        pending = ranges["shade"]
        if k + 1 < len(rounds):
            hear(k + 1)
            if k + 2 < len(rounds):
                tell(k + 2)

    for job in pending:
        shear_rows(*job)

    def tcopy(d):
        return pltpu.make_async_remote_copy(
            outbox.at[d], inbox.at[me], tsend, trecv, device_id=at(d, col)
        )

    def coded(x):
        return (jnp.sqrt(jnp.minimum(x, 1.0)) * 65535.0 + 0.5).astype(jnp.int32)

    full = 1.0625 * brightest
    per_full = 1.0 / full

    def march(d, box, slot):
        for v in range(2):
            tile = inverse[v, d]
            shaded, transmit = None, None
            for z in range(CZ) if v == 0 else range(CZ - 1, -1, -1):
                b = sheared[z, 0, tile, :, v * W : v * W + W]
                a = sheared[z, 1, tile, :, v * W : v * W + W]
                shaded = b if shaded is None else shaded + transmit * b
                transmit = 1.0 - a if transmit is None else transmit * (1.0 - a)
            box[slot, v] = (coded(shaded * per_full) << 16) | coded(1.0 - transmit)

    other = me + 1 - 2 * (me & 1)
    for j in range(G // 2 - 1):
        away = G // 4 + (j + 1) // 2 * (1 - 2 * (j % 2))
        chip = 2 * ((me // 2 + away) & (G // 2 - 1))
        pair = (chip + (me & 1), chip + 1 - (me & 1))
        for d in pair:
            march(d, outbox, d)
        for d in pair:
            tcopy(d).start()
    march(other, outbox, other)
    tcopy(other).start()
    march(me, inbox, me)

    others = pltpu.make_async_remote_copy(
        outbox.at[0 : G - 1], inbox.at[0 : G - 1], tsend, trecv, device_id=at(other, col)
    )
    for dz in (1, -1):
        @pl.when(has[dz])
        def _():
            for k in range(NC):
                zcopy(dz, k).wait_send()
    for dz, dr in rcopies:
        @pl.when(allowed(dz, dr))
        def _():
            rcopy(dz, dr).wait_send()
    others.wait_send()
    others.wait_recv()

    for v in range(2):
        def blend(i, carry):
            shaded, transmit = carry
            s = order_ref[v, i]
            word = inbox[s, v]
            c = ((word >> 16) & 65535).astype(F32) * (1.0 / 65535.0)
            a = (word & 65535).astype(F32) * (1.0 / 65535.0)
            return shaded + transmit * (c * c), transmit * (1.0 - a * a)

        shaded, transmit = lax.fori_loop(
            0, G, blend, (jnp.zeros((TR, W), F32), jnp.ones((TR, W), F32)), unroll=True
        )
        for c in range(3):
            out_ref[v, c] = shaded * (palette_ref[c] * 1.0625)
        out_ref[v, 3] = 1.0 - transmit


def solution(mesh):
    depth_axis, row_axis = mesh.axis_names
    G, R = mesh.shape[depth_axis], mesh.shape[row_axis]

    def body(density, live_slices, shear_slopes, palette, depth_order, tile_owner):
        CZ, CY, W = density.shape
        TR = CY // G
        arrays = (live_slices, shear_slopes, palette, depth_order, tile_owner, density)
        dma = pltpu.SemaphoreType.DMA
        NC = len(CHUNKS)
        out = pl.pallas_call(
            functools.partial(kernel, G, R, depth_axis, row_axis),
            out_shape=jax.ShapeDtypeStruct((2, 4, TR, W), F32),
            in_specs=[pl.BlockSpec(memory_space=pl.ANY)] * 6,
            out_specs=pl.BlockSpec(memory_space=pltpu.VMEM),
            scratch_shapes=[
                pltpu.VMEM((CZ, CY, W), F32),
                pltpu.VMEM((CZ, CY, W), F32),
                pltpu.VMEM((CZ, CY // 2, W), jnp.int32),
                pltpu.VMEM((2, 5, CY // 2, W), jnp.int32),
                pltpu.VMEM((2, CZ + 10, 8, W), F32),
                pltpu.VMEM((CZ + 2, CY + 16, W), F32),
                pltpu.VMEM((CZ + 2, CY + 8, W), F32),
                pltpu.VMEM((CZ + 2, CY + 8, W), F32),
                pltpu.VMEM((CZ + 2, CY + 8, W), F32),
                pltpu.VMEM((2 * W, 2 * W), BF16),
                pltpu.VMEM((CZ, 2, CY, W), BF16),
                pltpu.VMEM((CZ, W, 2 * W), BF16),
                pltpu.VMEM((CZ, 2, G, TR, 2 * W), F32),
                pltpu.VMEM((G, 2, TR, W), jnp.int32),
                pltpu.VMEM((G, 2, TR, W), jnp.int32),
                pltpu.SMEM((2, G), jnp.int32),
                *(pltpu.SMEM(a.shape, a.dtype) for a in arrays[:5]),
                dma((5,)),
                dma((NC,)),
                dma((2, NC)),
                dma((2, NC)),
                dma((2, 3)),
                dma((2, 3)),
                dma,
                dma,
                pltpu.SemaphoreType.REGULAR((3, 2)),
            ],
            compiler_params=pltpu.CompilerParams(collective_id=0, has_side_effects=True, vmem_limit_bytes=12 << 20),
        )(*(pltpu.with_memory_space_constraint(a, pltpu.HBM) for a in arrays))
        return out[:, :, None]

    placed = (P(depth_axis, row_axis, None), P(), P(), P(), P(), P())
    return jax.shard_map(
        body,
        mesh=mesh,
        in_specs=placed,
        out_specs=P(None, None, depth_axis, row_axis, None),
        check_vma=False,
    )
```

```python
import functools

import jax
import jax.numpy as jnp
from jax import lax
from jax.experimental import pallas as pl
from jax.experimental.pallas import tpu as pltpu
from jax.sharding import PartitionSpec as P

LIGHT = (0.48, 0.6, 0.64)
LOG2E = 1.4426950408889634
STEPS = 32767.0 / 96.0
CHUNKS = ((0, 32), (32, 80), (80, 128))
WORK = (
    {"rows": ((8, 32),), "shade": ()},
    {"rows": ((32, 80), (0, 8)), "shade": ((16, 64), (0, 16))},
    {"rows": ((80, 136),), "shade": ((64, 128),)},
)
F32, BF16 = jnp.float32, jnp.bfloat16


def spread(first, second, inside):
    return jnp.where(inside, jnp.where((first - second <= 4) & (second - first <= 4), 1.0, 0.0), 0.0)


def kernel(
    G, R, depth_axis, row_axis,
    live_hbm, slopes_hbm, palette_hbm, order_hbm, owner_hbm, dens_ref,
    out_ref,
    raw, quant, codes, halo, side_rows, summed, rowed, smooth, dcol, band, layers, shear, sheared, outbox, inbox, inverse, power,
    live_ref, slopes_ref, palette_ref, order_ref, owner_ref, table_sem, local_sem, zsend, zrecv, rsend, rrecv, tsend, trecv, known,
):
    me = lax.axis_index(depth_axis)
    col = lax.axis_index(row_axis)
    CZ, CY, W = dens_ref.shape
    TR = CY // G
    NC = len(CHUNKS)
    has = {-1: me > 0, 1: me < G - 1}
    hasr = {-1: col > 0, 1: col < R - 1}
    at = lambda g, r: {depth_axis: g, row_axis: r}

    barrier = pltpu.get_barrier_semaphore()

    def ring(k):
        return at(lax.rem(me + (k + G), G), col)

    for k in (-1, 1):
        pl.semaphore_signal(barrier, inc=1, device_id=ring(k))
    for dr in (-1, 1):
        for dz in (-1, 0, 1):
            ok = hasr[dr] if dz == 0 else hasr[dr] & has[dz]

            @pl.when(ok)
            def _():
                pl.semaphore_signal(barrier, inc=1, device_id=at(me + dz, col + dr))

    tables = [
        pltpu.make_async_copy(a, b, table_sem.at[i])
        for i, (a, b) in enumerate(
            (
                (owner_hbm, owner_ref), (slopes_hbm, slopes_ref), (live_hbm, live_ref),
                (palette_hbm, palette_ref), (order_hbm, order_ref),
            )
        )
    ]
    for table in tables:
        table.start()
    local = [
        pltpu.make_async_copy(dens_ref.at[:, lo:hi, :], raw.at[:, lo:hi, :], local_sem.at[k])
        for k, (lo, hi) in enumerate(CHUNKS)
    ]
    for part in local:
        part.start()

    def encode(k):
        lo, hi = CHUNKS[k]
        half = (hi - lo) // 2
        local[k].wait()
        for z in range(CZ):
            x = jnp.round(raw[z, lo:hi, :] * STEPS)
            quant[z, lo:hi, :] = x
            i = x.astype(jnp.int32)
            codes[z, lo // 2 : hi // 2, :] = (i[:half] << 16) + (i[half:] + 32768)

    for dz in (1, -1):
        @pl.when(jnp.logical_not(has[-dz]))
        def _():
            halo[(1 - dz) // 2] = jnp.full((5, CY // 2, W), 32768, jnp.int32)
            zd = slice(0, 5) if dz == 1 else slice(13, 18)
            side_rows[:, zd] = jnp.zeros((2, 5, 8, W), F32)
    for dr in (1, -1):
        @pl.when(jnp.logical_not(hasr[-dr]))
        def _():
            side_rows[(1 - dr) // 2] = jnp.zeros((CZ + 10, 8, W), F32)

    source = lax.broadcasted_iota(jnp.int32, (W, W), 0)
    target = lax.broadcasted_iota(jnp.int32, (W, W), 1)
    ones = spread(source, target, True)
    diff = spread(source, target + 1, target + 1 < W) - spread(source, target - 1, target >= 1)
    for half in range(2):
        band[half * W : half * W + W, 0:W] = ones.astype(BF16)
        band[half * W : half * W + W, W : 2 * W] = diff.astype(BF16)

    for table in tables:
        table.wait()

    offset = (source - target).astype(F32)

    def shears(z, carry):
        depth = (me * CZ + z).astype(F32) + (0.5 - 0.5 * CZ * G)
        for v in range(2):
            m = jnp.maximum(0.0, 1.0 - jnp.abs(offset + slopes_ref[v] * depth))
            shear[z, :, v * W : v * W + W] = m.astype(BF16)
        return carry

    lax.fori_loop(0, CZ, shears, 0)

    for d in range(G):
        for word in range(2):
            power[word, d] = jnp.int32(16 ** (d % 8) if d // 8 == word else 0)
    for v in range(2):
        for word in range(2):
            packed = jnp.int32(0)
            for t in range(1, G):
                packed = packed + t * power[word, owner_ref[v, t]]
            inverse[v, word] = packed

    encode(0)
    beside = hasr[-1].astype(jnp.int32) + hasr[1].astype(jnp.int32)
    above = has[-1].astype(jnp.int32) + has[1].astype(jnp.int32)
    pl.semaphore_wait(barrier, 2 + beside * (1 + above))

    rounds = [1 << j for j in range((G // 4).bit_length())]

    def tell(j):
        for side, sign in enumerate((1, -1)):
            pl.semaphore_signal(known.at[j, side], inc=1, device_id=ring(sign * rounds[j]))

    def hear(j):
        for side in range(2):
            pl.semaphore_wait(known.at[j, side], 1)

    def zcopy(dz, k):
        rows = slice(CHUNKS[k][0] // 2, CHUNKS[k][1] // 2)
        src = codes.at[3:8, rows, :] if dz == 1 else codes.at[0:5, rows, :]
        dst = halo.at[(1 - dz) // 2, :, rows, :]
        side = (dz + 1) // 2
        return pltpu.make_async_remote_copy(
            src, dst, zsend.at[side, k], zrecv.at[side, k], device_id=at(me + dz, col)
        )

    def rcopy(dz, dr):
        zs, zd = {0: (slice(0, 8), slice(5, 13)), 1: (slice(3, 8), slice(0, 5)), -1: (slice(0, 5), slice(13, 18))}[dz]
        rs, rd = {1: (slice(120, 128), 0), -1: (slice(0, 8), 1)}[dr]
        side = (dr + 1) // 2
        return pltpu.make_async_remote_copy(
            dens_ref.at[zs, rs, :], side_rows.at[rd, zd], rsend.at[side, dz + 1], rrecv.at[side, dz + 1],
            device_id=at(me + dz, col + dr),
        )

    zcopies = [(dz, k) for k in range(NC) for dz in (1, -1)]
    rcopies = [(dz, dr) for dr in (-1, 1) for dz in (1, -1, 0)]

    def allowed(dz, dr):
        return hasr[dr] if dz == 0 else hasr[dr] & has[dz]

    tell(0)
    for dz in (1, -1):
        @pl.when(has[dz])
        def _():
            zcopy(dz, 0).start()
    for dz, dr in rcopies:
        @pl.when(allowed(dz, dr))
        def _():
            rcopy(dz, dr).start()
    for k in range(1, NC):
        encode(k)
        for dz in (1, -1):
            @pl.when(has[dz])
            def _():
                zcopy(dz, k).start()

    live = live_ref[me, col]
    brightest = jnp.maximum(jnp.maximum(palette_ref[0], palette_ref[1]), palette_ref[2])

    ambient = 0.25 * brightest
    light = [0.75 * part * brightest for part in LIGHT]
    rate = -3.0 * LOG2E / (CZ * G)

    def depth_sum(x, q):
        two = [x[i] + x[i + 1] for i in range(CZ + 8)]
        four = [two[i] + two[i + 2] for i in range(CZ + 6)]
        eight = [four[i] + four[i + 4] for i in range(CZ + 2)]
        for z in range(CZ + 2):
            summed[z, q : q + 8, :] = eight[z] + x[z + 8]

    def depth_sums(k):
        lo, hi = CHUNKS[k]
        half = (hi - lo) // 2
        for b in range(0, half, 8):
            words = [[halo[side, z, lo // 2 + b : lo // 2 + b + 8, :] for z in range(5)] for side in range(2)]
            for part in range(2):
                r = lo + part * half + b
                below, above = [
                    [((w >> 16) if part == 0 else (w & 65535) - 32768).astype(F32) for w in ws] for ws in words
                ]
                depth_sum(below + [quant[z, r : r + 8, :] for z in range(CZ)] + above, r + 8)

    def side_sums(side):
        x = [jnp.round(side_rows[side, z] * STEPS) for z in range(CZ + 10)]
        depth_sum(x, side * (CY + 8))

    def smooth_rows(lo, hi):
        def layer(z, carry):
            for j in range(lo, hi, 8):
                s = [summed[z, j + k : j + 8 + k, :] for k in range(9)]
                rowed[z, j : j + 8, :] = (
                    ((s[0] + s[1]) + (s[2] + s[3])) + ((s[4] + s[5]) + (s[6] + s[7])) + s[8]
                )
            return carry

        lax.fori_loop(0, CZ + 2, layer, 0, unroll=True)

    def smooth_cols(lo, hi):
        n = (CZ + 2) * (hi - lo)
        x = rowed[:, lo:hi, :].reshape(n, W)
        high = x.astype(BF16)
        low = (x - high.astype(F32)).astype(BF16)
        both = jnp.dot(
            jnp.concatenate([high, low], axis=1), band[...], preferred_element_type=F32
        )
        smooth[:, lo:hi, :] = both[:, 0:W].reshape(CZ + 2, hi - lo, W)
        dcol[:, lo:hi, :] = both[:, W : 2 * W].reshape(CZ + 2, hi - lo, W)

    def shade(lo, hi):
        def layer(z, carry):
            fade = rate * (z < live).astype(jnp.int32).astype(F32)
            for r in range(lo, hi, 16):
                q = r + 4
                n = 16
                center = smooth[z + 1, q : q + n, :]
                dz = smooth[z + 2, q : q + n, :] - smooth[z, q : q + n, :]
                dr = smooth[z + 1, q + 1 : q + n + 1, :] - smooth[z + 1, q - 1 : q + n - 1, :]
                dc = dcol[z + 1, q : q + n, :]
                along = jnp.maximum(0.0, light[0] * dz + light[1] * dr + light[2] * dc)
                lit = ambient + along * lax.rsqrt((dz * dz + 0.01 * (1458.0 * STEPS) ** 2) + (dr * dr + dc * dc))
                soft = jnp.maximum(center * (2.0 / (729.0 * STEPS)), 0.0) + jnp.log(
                    1.0 + jnp.exp2(jnp.abs(center) * (-2.0 * LOG2E / (729.0 * STEPS)))
                )
                opacity = 1.0 - jnp.exp2(soft * fade)
                layers[z, 0, r : r + n, :] = (opacity * lit).astype(BF16)
                layers[z, 1, r : r + n, :] = opacity.astype(BF16)
            return carry

        lax.fori_loop(0, CZ, layer, 0, unroll=True)

    def shear_rows(lo, hi):
        for z in range(CZ):
            lhs = layers[z, :, lo:hi, :].reshape(2 * (hi - lo), W)
            out = jnp.dot(lhs, shear[z], preferred_element_type=F32)
            sheared[z, :, lo // TR : hi // TR] = out.reshape(2, (hi - lo) // TR, TR, 2 * W)

    def clear(lo, hi):
        for dz in (-1, 1):
            @pl.when(jnp.logical_not(has[dz]))
            def _():
                smooth[0 if dz == -1 else CZ + 1, lo:hi, :] = jnp.zeros((hi - lo, W), F32)

    hear(0)
    if len(rounds) > 1:
        tell(1)
    def sides_in(dr):
        for dz in (1, -1, 0):
            @pl.when(allowed(-dz, -dr))
            def _():
                rcopy(dz, dr).wait_recv()

    pending = []
    for k, ranges in enumerate(WORK):
        for dz in (1, -1):
            @pl.when(has[-dz])
            def _():
                zcopy(dz, k).wait_recv()
        depth_sums(k)
        if ranges["rows"][-1][0] == 0:
            sides_in(1)
            side_sums(0)
        if ranges["rows"][-1][1] == CY + 8:
            sides_in(-1)
            side_sums(1)
        for first, end in ranges["rows"]:
            smooth_rows(first, end)
        for job in pending:
            shear_rows(*job)
        for first, end in ranges["rows"]:
            smooth_cols(first, end)
            clear(first, end)
            if first == 0:
                @pl.when(jnp.logical_not(hasr[-1]))
                def _():
                    smooth[:, 0:4, :] = jnp.zeros((CZ + 2, 4, W), F32)
            if end == CY + 8:
                @pl.when(jnp.logical_not(hasr[1]))
                def _():
                    smooth[:, CY + 4 : CY + 8, :] = jnp.zeros((CZ + 2, 4, W), F32)
        for job in ranges["shade"]:
            shade(*job)
        pending = ranges["shade"]
        if k + 1 < len(rounds):
            hear(k + 1)
            if k + 2 < len(rounds):
                tell(k + 2)

    for job in pending:
        shear_rows(*job)

    def tcopy(d):
        return pltpu.make_async_remote_copy(
            outbox.at[d], inbox.at[me], tsend, trecv, device_id=at(d, col)
        )

    def coded(x):
        return (jnp.sqrt(jnp.minimum(x, 1.0)) * 65535.0 + 0.5).astype(jnp.int32)

    full = 1.0625 * brightest
    per_full = 1.0 / full

    def march(d, box, slot):
        for v in range(2):
            tile = (inverse[v, d // 8] >> (4 * (d & 7))) & 15
            shaded, transmit = None, None
            for z in range(CZ) if v == 0 else range(CZ - 1, -1, -1):
                b = sheared[z, 0, tile, :, v * W : v * W + W]
                a = sheared[z, 1, tile, :, v * W : v * W + W]
                shaded = b if shaded is None else shaded + transmit * b
                transmit = 1.0 - a if transmit is None else transmit * (1.0 - a)
            box[slot, v] = (coded(shaded * per_full) << 16) | coded(1.0 - transmit)

    other = me + 1 - 2 * (me & 1)
    for j in range(G // 2 - 1):
        away = G // 4 + (j + 1) // 2 * (1 - 2 * (j % 2))
        chip = 2 * ((me // 2 + away) & (G // 2 - 1))
        pair = (chip + (me & 1), chip + 1 - (me & 1))
        for d in pair:
            march(d, outbox, d)
        for d in pair:
            tcopy(d).start()
    march(other, outbox, other)
    tcopy(other).start()
    march(me, inbox, me)

    others = pltpu.make_async_remote_copy(
        outbox.at[0 : G - 1], inbox.at[0 : G - 1], tsend, trecv, device_id=at(other, col)
    )
    for dz in (1, -1):
        @pl.when(has[dz])
        def _():
            for k in range(NC):
                zcopy(dz, k).wait_send()
    for dz, dr in rcopies:
        @pl.when(allowed(dz, dr))
        def _():
            rcopy(dz, dr).wait_send()
    others.wait_send()
    others.wait_recv()

    for v in range(2):
        def blend(i, carry):
            shaded, transmit = carry
            s = order_ref[v, i]
            word = inbox[s, v]
            c = ((word >> 16) & 65535).astype(F32) * (1.0 / 65535.0)
            a = (word & 65535).astype(F32) * (1.0 / 65535.0)
            return shaded + transmit * (c * c), transmit * (1.0 - a * a)

        shaded, transmit = lax.fori_loop(
            0, G, blend, (jnp.zeros((TR, W), F32), jnp.ones((TR, W), F32)), unroll=True
        )
        for c in range(3):
            out_ref[v, c] = shaded * (palette_ref[c] * 1.0625)
        out_ref[v, 3] = 1.0 - transmit


def solution(mesh):
    depth_axis, row_axis = mesh.axis_names
    G, R = mesh.shape[depth_axis], mesh.shape[row_axis]

    def body(density, live_slices, shear_slopes, palette, depth_order, tile_owner):
        CZ, CY, W = density.shape
        TR = CY // G
        arrays = (live_slices, shear_slopes, palette, depth_order, tile_owner, density)
        dma = pltpu.SemaphoreType.DMA
        NC = len(CHUNKS)
        out = pl.pallas_call(
            functools.partial(kernel, G, R, depth_axis, row_axis),
            out_shape=jax.ShapeDtypeStruct((2, 4, TR, W), F32),
            in_specs=[pl.BlockSpec(memory_space=pl.ANY)] * 6,
            out_specs=pl.BlockSpec(memory_space=pltpu.VMEM),
            scratch_shapes=[
                pltpu.VMEM((CZ, CY, W), F32),
                pltpu.VMEM((CZ, CY, W), F32),
                pltpu.VMEM((CZ, CY // 2, W), jnp.int32),
                pltpu.VMEM((2, 5, CY // 2, W), jnp.int32),
                pltpu.VMEM((2, CZ + 10, 8, W), F32),
                pltpu.VMEM((CZ + 2, CY + 16, W), F32),
                pltpu.VMEM((CZ + 2, CY + 8, W), F32),
                pltpu.VMEM((CZ + 2, CY + 8, W), F32),
                pltpu.VMEM((CZ + 2, CY + 8, W), F32),
                pltpu.VMEM((2 * W, 2 * W), BF16),
                pltpu.VMEM((CZ, 2, CY, W), BF16),
                pltpu.VMEM((CZ, W, 2 * W), BF16),
                pltpu.VMEM((CZ, 2, G, TR, 2 * W), F32),
                pltpu.VMEM((G, 2, TR, W), jnp.int32),
                pltpu.VMEM((G, 2, TR, W), jnp.int32),
                pltpu.SMEM((2, 2), jnp.int32),
                pltpu.SMEM((2, G), jnp.int32),
                *(pltpu.SMEM(a.shape, a.dtype) for a in arrays[:5]),
                dma((5,)),
                dma((NC,)),
                dma((2, NC)),
                dma((2, NC)),
                dma((2, 3)),
                dma((2, 3)),
                dma,
                dma,
                pltpu.SemaphoreType.REGULAR((3, 2)),
            ],
            compiler_params=pltpu.CompilerParams(collective_id=0, has_side_effects=True, vmem_limit_bytes=12 << 20),
        )(*(pltpu.with_memory_space_constraint(a, pltpu.HBM) for a in arrays))
        return out[:, :, None]

    placed = (P(depth_axis, row_axis, None), P(), P(), P(), P(), P())
    return jax.shard_map(
        body,
        mesh=mesh,
        in_specs=placed,
        out_specs=P(None, None, depth_axis, row_axis, None),
        check_vma=False,
    )
```

```python
import functools

import jax
import jax.numpy as jnp
from jax import lax
from jax.experimental import pallas as pl
from jax.experimental.pallas import tpu as pltpu
from jax.sharding import PartitionSpec as P

LIGHT = (0.48, 0.6, 0.64)
LOG2E = 1.4426950408889634
STEPS = 32767.0 / 96.0
CHUNKS = ((0, 32), (32, 80), (80, 128))
WORK = (
    {"rows": ((8, 32),), "shade": ()},
    {"rows": ((32, 80), (0, 8)), "shade": ((16, 64), (0, 16))},
    {"rows": ((80, 136),), "shade": ((64, 128),)},
)
F32, BF16 = jnp.float32, jnp.bfloat16


def spread(first, second, inside):
    return jnp.where(inside, jnp.where((first - second <= 4) & (second - first <= 4), 1.0, 0.0), 0.0)


def kernel(
    G, R, depth_axis, row_axis,
    live_hbm, slopes_hbm, palette_hbm, order_hbm, owner_hbm, dens_ref,
    out_ref,
    raw, quant, codes, halo, side_rows, summed, rowed, smooth, dcol, band, layers, shear, sheared, outbox, inbox, inverse, power,
    live_ref, slopes_ref, palette_ref, order_ref, owner_ref, table_sem, local_sem, zsend, zrecv, rsend, rrecv, tsend, trecv, known,
):
    me = lax.axis_index(depth_axis)
    col = lax.axis_index(row_axis)
    CZ, CY, W = dens_ref.shape
    TR = CY // G
    NC = len(CHUNKS)
    has = {-1: me > 0, 1: me < G - 1}
    hasr = {-1: col > 0, 1: col < R - 1}
    at = lambda g, r: {depth_axis: g, row_axis: r}

    barrier = pltpu.get_barrier_semaphore()

    def ring(k):
        return at(lax.rem(me + (k + G), G), col)

    for k in (-1, 1):
        pl.semaphore_signal(barrier, inc=1, device_id=ring(k))
    for dr in (-1, 1):
        for dz in (-1, 0, 1):
            ok = hasr[dr] if dz == 0 else hasr[dr] & has[dz]

            @pl.when(ok)
            def _():
                pl.semaphore_signal(barrier, inc=1, device_id=at(me + dz, col + dr))

    tables = [
        pltpu.make_async_copy(a, b, table_sem.at[i])
        for i, (a, b) in enumerate(
            (
                (owner_hbm, owner_ref), (slopes_hbm, slopes_ref), (live_hbm, live_ref),
                (palette_hbm, palette_ref), (order_hbm, order_ref),
            )
        )
    ]
    for table in tables:
        table.start()
    local = [
        pltpu.make_async_copy(dens_ref.at[:, lo:hi, :], raw.at[:, lo:hi, :], local_sem.at[k])
        for k, (lo, hi) in enumerate(CHUNKS)
    ]
    for part in local:
        part.start()

    def encode(k):
        lo, hi = CHUNKS[k]
        half = (hi - lo) // 2
        local[k].wait()
        for z in range(CZ):
            x = jnp.round(raw[z, lo:hi, :] * STEPS)
            quant[z, lo:hi, :] = x
            i = x.astype(jnp.int32)
            codes[z, lo // 2 : hi // 2, :] = (i[:half] << 16) + (i[half:] + 32768)

    for dz in (1, -1):
        @pl.when(jnp.logical_not(has[-dz]))
        def _():
            halo[(1 - dz) // 2] = jnp.full((5, CY // 2, W), 32768, jnp.int32)
            zd = slice(0, 5) if dz == 1 else slice(13, 18)
            side_rows[:, zd] = jnp.zeros((2, 5, 8, W), F32)
    for dr in (1, -1):
        @pl.when(jnp.logical_not(hasr[-dr]))
        def _():
            side_rows[(1 - dr) // 2] = jnp.zeros((CZ + 10, 8, W), F32)

    source = lax.broadcasted_iota(jnp.int32, (W, W), 0)
    target = lax.broadcasted_iota(jnp.int32, (W, W), 1)
    ones = spread(source, target, True)
    diff = spread(source, target + 1, target + 1 < W) - spread(source, target - 1, target >= 1)
    for half in range(2):
        band[half * W : half * W + W, 0:W] = ones.astype(BF16)
        band[half * W : half * W + W, W : 2 * W] = diff.astype(BF16)

    encode(0)
    beside = hasr[-1].astype(jnp.int32) + hasr[1].astype(jnp.int32)
    above = has[-1].astype(jnp.int32) + has[1].astype(jnp.int32)
    pl.semaphore_wait(barrier, 2 + beside * (1 + above))

    rounds = [1 << j for j in range((G // 4).bit_length())]

    def tell(j):
        for side, sign in enumerate((1, -1)):
            pl.semaphore_signal(known.at[j, side], inc=1, device_id=ring(sign * rounds[j]))

    def hear(j):
        for side in range(2):
            pl.semaphore_wait(known.at[j, side], 1)

    def zcopy(dz, k):
        rows = slice(CHUNKS[k][0] // 2, CHUNKS[k][1] // 2)
        src = codes.at[3:8, rows, :] if dz == 1 else codes.at[0:5, rows, :]
        dst = halo.at[(1 - dz) // 2, :, rows, :]
        side = (dz + 1) // 2
        return pltpu.make_async_remote_copy(
            src, dst, zsend.at[side, k], zrecv.at[side, k], device_id=at(me + dz, col)
        )

    def rcopy(dz, dr):
        zs, zd = {0: (slice(0, 8), slice(5, 13)), 1: (slice(3, 8), slice(0, 5)), -1: (slice(0, 5), slice(13, 18))}[dz]
        rs, rd = {1: (slice(120, 128), 0), -1: (slice(0, 8), 1)}[dr]
        side = (dr + 1) // 2
        return pltpu.make_async_remote_copy(
            dens_ref.at[zs, rs, :], side_rows.at[rd, zd], rsend.at[side, dz + 1], rrecv.at[side, dz + 1],
            device_id=at(me + dz, col + dr),
        )

    zcopies = [(dz, k) for k in range(NC) for dz in (1, -1)]
    rcopies = [(dz, dr) for dr in (-1, 1) for dz in (1, -1, 0)]

    def allowed(dz, dr):
        return hasr[dr] if dz == 0 else hasr[dr] & has[dz]

    tell(0)
    for dz in (1, -1):
        @pl.when(has[dz])
        def _():
            zcopy(dz, 0).start()
    for dz, dr in rcopies:
        @pl.when(allowed(dz, dr))
        def _():
            rcopy(dz, dr).start()
    for k in range(1, NC):
        encode(k)
        for dz in (1, -1):
            @pl.when(has[dz])
            def _():
                zcopy(dz, k).start()

    for table in tables:
        table.wait()

    offset = (source - target).astype(F32)

    def shears(z, carry):
        depth = (me * CZ + z).astype(F32) + (0.5 - 0.5 * CZ * G)
        for v in range(2):
            m = jnp.maximum(0.0, 1.0 - jnp.abs(offset + slopes_ref[v] * depth))
            shear[z, :, v * W : v * W + W] = m.astype(BF16)
        return carry

    lax.fori_loop(0, CZ, shears, 0)

    for d in range(G):
        for word in range(2):
            power[word, d] = jnp.int32(16 ** (d % 8) if d // 8 == word else 0)
    for v in range(2):
        for word in range(2):
            packed = jnp.int32(0)
            for t in range(1, G):
                packed = packed + t * power[word, owner_ref[v, t]]
            inverse[v, word] = packed

    live = live_ref[me, col]
    brightest = jnp.maximum(jnp.maximum(palette_ref[0], palette_ref[1]), palette_ref[2])

    ambient = 0.25 * brightest
    light = [0.75 * part * brightest for part in LIGHT]
    rate = -3.0 * LOG2E / (CZ * G)

    def depth_sum(x, q):
        two = [x[i] + x[i + 1] for i in range(CZ + 8)]
        four = [two[i] + two[i + 2] for i in range(CZ + 6)]
        eight = [four[i] + four[i + 4] for i in range(CZ + 2)]
        for z in range(CZ + 2):
            summed[z, q : q + 8, :] = eight[z] + x[z + 8]

    def depth_sums(k):
        lo, hi = CHUNKS[k]
        half = (hi - lo) // 2
        for b in range(0, half, 8):
            words = [[halo[side, z, lo // 2 + b : lo // 2 + b + 8, :] for z in range(5)] for side in range(2)]
            for part in range(2):
                r = lo + part * half + b
                below, above = [
                    [((w >> 16) if part == 0 else (w & 65535) - 32768).astype(F32) for w in ws] for ws in words
                ]
                depth_sum(below + [quant[z, r : r + 8, :] for z in range(CZ)] + above, r + 8)

    def side_sums(side):
        x = [jnp.round(side_rows[side, z] * STEPS) for z in range(CZ + 10)]
        depth_sum(x, side * (CY + 8))

    def smooth_rows(lo, hi):
        def layer(z, carry):
            for j in range(lo, hi, 8):
                s = [summed[z, j + k : j + 8 + k, :] for k in range(9)]
                rowed[z, j : j + 8, :] = (
                    ((s[0] + s[1]) + (s[2] + s[3])) + ((s[4] + s[5]) + (s[6] + s[7])) + s[8]
                )
            return carry

        lax.fori_loop(0, CZ + 2, layer, 0, unroll=True)

    def smooth_cols(lo, hi):
        n = (CZ + 2) * (hi - lo)
        x = rowed[:, lo:hi, :].reshape(n, W)
        high = x.astype(BF16)
        low = (x - high.astype(F32)).astype(BF16)
        both = jnp.dot(
            jnp.concatenate([high, low], axis=1), band[...], preferred_element_type=F32
        )
        smooth[:, lo:hi, :] = both[:, 0:W].reshape(CZ + 2, hi - lo, W)
        dcol[:, lo:hi, :] = both[:, W : 2 * W].reshape(CZ + 2, hi - lo, W)

    def shade(lo, hi):
        def layer(z, carry):
            fade = rate * (z < live).astype(jnp.int32).astype(F32)
            for r in range(lo, hi, 16):
                q = r + 4
                n = 16
                center = smooth[z + 1, q : q + n, :]
                dz = smooth[z + 2, q : q + n, :] - smooth[z, q : q + n, :]
                dr = smooth[z + 1, q + 1 : q + n + 1, :] - smooth[z + 1, q - 1 : q + n - 1, :]
                dc = dcol[z + 1, q : q + n, :]
                along = jnp.maximum(0.0, light[0] * dz + light[1] * dr + light[2] * dc)
                lit = ambient + along * lax.rsqrt((dz * dz + 0.01 * (1458.0 * STEPS) ** 2) + (dr * dr + dc * dc))
                soft = jnp.maximum(center * (2.0 / (729.0 * STEPS)), 0.0) + jnp.log(
                    1.0 + jnp.exp2(jnp.abs(center) * (-2.0 * LOG2E / (729.0 * STEPS)))
                )
                opacity = 1.0 - jnp.exp2(soft * fade)
                layers[z, 0, r : r + n, :] = (opacity * lit).astype(BF16)
                layers[z, 1, r : r + n, :] = opacity.astype(BF16)
            return carry

        lax.fori_loop(0, CZ, layer, 0, unroll=True)

    def shear_rows(lo, hi):
        for z in range(CZ):
            lhs = layers[z, :, lo:hi, :].reshape(2 * (hi - lo), W)
            out = jnp.dot(lhs, shear[z], preferred_element_type=F32)
            sheared[z, :, lo // TR : hi // TR] = out.reshape(2, (hi - lo) // TR, TR, 2 * W)

    def clear(lo, hi):
        for dz in (-1, 1):
            @pl.when(jnp.logical_not(has[dz]))
            def _():
                smooth[0 if dz == -1 else CZ + 1, lo:hi, :] = jnp.zeros((hi - lo, W), F32)

    hear(0)
    if len(rounds) > 1:
        tell(1)
    def sides_in(dr):
        for dz in (1, -1, 0):
            @pl.when(allowed(-dz, -dr))
            def _():
                rcopy(dz, dr).wait_recv()

    pending = []
    for k, ranges in enumerate(WORK):
        for dz in (1, -1):
            @pl.when(has[-dz])
            def _():
                zcopy(dz, k).wait_recv()
        depth_sums(k)
        if ranges["rows"][-1][0] == 0:
            sides_in(1)
            side_sums(0)
        if ranges["rows"][-1][1] == CY + 8:
            sides_in(-1)
            side_sums(1)
        for first, end in ranges["rows"]:
            smooth_rows(first, end)
        for job in pending:
            shear_rows(*job)
        for first, end in ranges["rows"]:
            smooth_cols(first, end)
            clear(first, end)
            if first == 0:
                @pl.when(jnp.logical_not(hasr[-1]))
                def _():
                    smooth[:, 0:4, :] = jnp.zeros((CZ + 2, 4, W), F32)
            if end == CY + 8:
                @pl.when(jnp.logical_not(hasr[1]))
                def _():
                    smooth[:, CY + 4 : CY + 8, :] = jnp.zeros((CZ + 2, 4, W), F32)
        for job in ranges["shade"]:
            shade(*job)
        pending = ranges["shade"]
        if k + 1 < len(rounds):
            hear(k + 1)
            if k + 2 < len(rounds):
                tell(k + 2)

    for job in pending:
        shear_rows(*job)

    def tcopy(d):
        return pltpu.make_async_remote_copy(
            outbox.at[d], inbox.at[me], tsend, trecv, device_id=at(d, col)
        )

    def coded(x):
        return (jnp.sqrt(jnp.minimum(x, 1.0)) * 65535.0 + 0.5).astype(jnp.int32)

    full = 1.0625 * brightest
    per_full = 1.0 / full

    def march(d, box, slot):
        for v in range(2):
            tile = (inverse[v, d // 8] >> (4 * (d & 7))) & 15
            shaded, transmit = None, None
            for z in range(CZ) if v == 0 else range(CZ - 1, -1, -1):
                b = sheared[z, 0, tile, :, v * W : v * W + W]
                a = sheared[z, 1, tile, :, v * W : v * W + W]
                shaded = b if shaded is None else shaded + transmit * b
                transmit = 1.0 - a if transmit is None else transmit * (1.0 - a)
            box[slot, v] = (coded(shaded * per_full) << 16) | coded(1.0 - transmit)

    other = me + 1 - 2 * (me & 1)
    for j in range(G // 2 - 1):
        away = G // 4 + (j + 1) // 2 * (1 - 2 * (j % 2))
        chip = 2 * ((me // 2 + away) & (G // 2 - 1))
        pair = (chip + (me & 1), chip + 1 - (me & 1))
        for d in pair:
            march(d, outbox, d)
        for d in pair:
            tcopy(d).start()
    march(other, outbox, other)
    tcopy(other).start()
    march(me, inbox, me)

    others = pltpu.make_async_remote_copy(
        outbox.at[0 : G - 1], inbox.at[0 : G - 1], tsend, trecv, device_id=at(other, col)
    )
    for dz in (1, -1):
        @pl.when(has[dz])
        def _():
            for k in range(NC):
                zcopy(dz, k).wait_send()
    for dz, dr in rcopies:
        @pl.when(allowed(dz, dr))
        def _():
            rcopy(dz, dr).wait_send()
    others.wait_send()
    others.wait_recv()

    for v in range(2):
        def blend(i, carry):
            shaded, transmit = carry
            s = order_ref[v, i]
            word = inbox[s, v]
            c = ((word >> 16) & 65535).astype(F32) * (1.0 / 65535.0)
            a = (word & 65535).astype(F32) * (1.0 / 65535.0)
            return shaded + transmit * (c * c), transmit * (1.0 - a * a)

        shaded, transmit = lax.fori_loop(
            0, G, blend, (jnp.zeros((TR, W), F32), jnp.ones((TR, W), F32)), unroll=True
        )
        for c in range(3):
            out_ref[v, c] = shaded * (palette_ref[c] * 1.0625)
        out_ref[v, 3] = 1.0 - transmit


def solution(mesh):
    depth_axis, row_axis = mesh.axis_names
    G, R = mesh.shape[depth_axis], mesh.shape[row_axis]

    def body(density, live_slices, shear_slopes, palette, depth_order, tile_owner):
        CZ, CY, W = density.shape
        TR = CY // G
        arrays = (live_slices, shear_slopes, palette, depth_order, tile_owner, density)
        dma = pltpu.SemaphoreType.DMA
        NC = len(CHUNKS)
        out = pl.pallas_call(
            functools.partial(kernel, G, R, depth_axis, row_axis),
            out_shape=jax.ShapeDtypeStruct((2, 4, TR, W), F32),
            in_specs=[pl.BlockSpec(memory_space=pl.ANY)] * 6,
            out_specs=pl.BlockSpec(memory_space=pltpu.VMEM),
            scratch_shapes=[
                pltpu.VMEM((CZ, CY, W), F32),
                pltpu.VMEM((CZ, CY, W), F32),
                pltpu.VMEM((CZ, CY // 2, W), jnp.int32),
                pltpu.VMEM((2, 5, CY // 2, W), jnp.int32),
                pltpu.VMEM((2, CZ + 10, 8, W), F32),
                pltpu.VMEM((CZ + 2, CY + 16, W), F32),
                pltpu.VMEM((CZ + 2, CY + 8, W), F32),
                pltpu.VMEM((CZ + 2, CY + 8, W), F32),
                pltpu.VMEM((CZ + 2, CY + 8, W), F32),
                pltpu.VMEM((2 * W, 2 * W), BF16),
                pltpu.VMEM((CZ, 2, CY, W), BF16),
                pltpu.VMEM((CZ, W, 2 * W), BF16),
                pltpu.VMEM((CZ, 2, G, TR, 2 * W), F32),
                pltpu.VMEM((G, 2, TR, W), jnp.int32),
                pltpu.VMEM((G, 2, TR, W), jnp.int32),
                pltpu.SMEM((2, 2), jnp.int32),
                pltpu.SMEM((2, G), jnp.int32),
                *(pltpu.SMEM(a.shape, a.dtype) for a in arrays[:5]),
                dma((5,)),
                dma((NC,)),
                dma((2, NC)),
                dma((2, NC)),
                dma((2, 3)),
                dma((2, 3)),
                dma,
                dma,
                pltpu.SemaphoreType.REGULAR((3, 2)),
            ],
            compiler_params=pltpu.CompilerParams(collective_id=0, has_side_effects=True, vmem_limit_bytes=12 << 20),
        )(*(pltpu.with_memory_space_constraint(a, pltpu.HBM) for a in arrays))
        return out[:, :, None]

    placed = (P(depth_axis, row_axis, None), P(), P(), P(), P(), P())
    return jax.shard_map(
        body,
        mesh=mesh,
        in_specs=placed,
        out_specs=P(None, None, depth_axis, row_axis, None),
        check_vma=False,
    )
```
